128 devices in a mesh: dp: 4 (over z), table: 32 (over x, y, core).
Axes of the slice: x: 4, y: 4, z: 4, core: 2. Of those that a mesh axis runs over, the one named last changes fastest.
Arguments:
- core_ids: int32 [16384, 32, 3, 2], P(('dp', 'table')), may hold values from 0 to 249
- bag_lengths: int32 [16384, 32], P(('dp', 'table')), may hold values from 1 to 2
- first_core: bfloat16 [32, 250, 512], P('table'), may hold values from -6 to 6
- middle_core: bfloat16 [32, 250, 64, 128], P('table'), may hold values from -0.75 to 0.75
- last_core: bfloat16 [32, 250, 512], P('table'), may hold values from -0.75 to 0.75
- grad_hidden: bfloat16 [16384, 1024], P(('dp', 'table')), may hold values from -0.1875 to 0.1875
Outputs:
- pooled: bfloat16 [16384, 4096], P(('dp', 'table'))
- weight_grad: float32 [4096, 1024], P('table', 'dp')
The draws below stay inside these ranges and needn't reach their ends.
Inputs may be any that keep to these rules, and one draw needn't show every extreme that they name: `core_ids`: slots j >= bag_lengths[n, t] hold ids that are not used.
All inputs are finite; a program needn't handle non-finite values.
Results may differ from the reference program's by a relative error of at most 0.005.
Values may be sent and summed in bfloat16 or wider, within the bound.
No kernel may reach another device: no remote copies, remote signals or barrier semaphores. Data moves between devices by JAX's collectives and lax.ppermute only.
A program may use at most 128 MiB of HBM per device.

```python
import jax
import jax.numpy as jnp
from jax import lax

D1 = 8
D2 = 2
D3 = 8
RANK = 64
NCORE = 250
HID = 1024
BAG = 2
TABLES = 32
BATCH = 16384


def set_ends(entries, rng, least, high):
    dims = entries.shape
    spot = [jax.random.randint(jax.random.fold_in(rng, axis), (), 0, dims[axis]) for axis in range(len(dims))]
    entries = entries.at[tuple(spot)].set(least)
    longest = dims.index(max(dims))
    spot[longest] = (spot[longest] + 1) % dims[longest]
    return entries.at[tuple(spot)].set(high)


def raised(entries, key, source, target, parts, factor):
    owner, partner = [(jnp.arange(entries.shape[dim]) // (entries.shape[dim] // parts)).reshape([-1 if axis == dim else 1 for axis in range(entries.ndim)]) for dim in (source, target)]
    chosen = jax.random.permutation(key, parts)[partner]
    strong = (owner == chosen) | (owner == (partner + parts // 2) % parts)
    return jnp.where(strong, factor * entries, entries)


def level_of(key, extent, pieces, smallest, largest):
    loudness = 1.0
    for dim, blocks in pieces:
        draws = jax.random.uniform(jax.random.fold_in(jax.random.fold_in(key, 6), dim), (blocks,), jnp.float32, smallest / len(pieces), largest / len(pieces))
        loudness = loudness * jnp.repeat(jnp.exp(draws), extent[dim] // blocks).reshape((-1,) + (1,) * (len(extent) - 1 - dim))
    return loudness


def centred(own_key, dims, width, limit, pieces=(), kind=jnp.bfloat16):
    array = jax.random.normal(own_key, dims, jnp.float32) * width
    if len(pieces) > 0:
        array = level_of(own_key, dims, pieces, -0.22, 0.18) * array
    return jnp.clip(array, min=-limit, max=limit).astype(kind)


def heavy_noise(key, shape, scale, limit, pieces, heavy, kind=jnp.bfloat16):
    entries = scale * jax.random.normal(key, shape, jnp.float32)
    if pieces:
        entries = entries * level_of(key, shape, pieces, -0.22, 0.18)
    return jnp.clip(raised(entries, jax.random.fold_in(key, 3), *heavy), -limit, limit).astype(kind)


def setup_inputs(seed: int = 0) -> dict:
    streams_of = jax.random.split(jax.random.key(seed), 7)
    return {
        "core_ids": set_ends(jax.random.randint(streams_of[0], (BATCH, TABLES, 3, BAG), 0, NCORE), jax.random.fold_in(streams_of[0], 1), 0, NCORE - 1).astype(jnp.int32),
        "bag_lengths": set_ends(jax.random.randint(streams_of[1], (BATCH, TABLES), 1, BAG + 1), jax.random.fold_in(streams_of[1], 1), 1, BAG).astype(jnp.int32),
        "first_core": centred(streams_of[2], (TABLES, NCORE, D1 * RANK), 1.0, 6.0, ((0, 32),)),
        "middle_core": centred(streams_of[3], (TABLES, NCORE, RANK, D2 * RANK), RANK ** -0.5, 0.75, ((0, 32),)),
        "last_core": centred(streams_of[4], (TABLES, NCORE, RANK * D3), RANK ** -0.5, 0.75, ((0, 32),)),
        "grad_hidden": heavy_noise(streams_of[5], (BATCH, HID), BATCH ** -0.5, 0.1875, ((0, 128),), (0, 1, 128, 5.5)),
    }


def build_rows(wanted, counts, first, middle, last):
    block = wanted.shape[0]
    head = jnp.take(first, wanted[:, 0, :], axis=0).astype(jnp.float32).reshape(block, BAG, D1, RANK)
    centre = jnp.take(middle, wanted[:, 1, :], axis=0).astype(jnp.float32)
    prefix = jnp.einsum('njar,njrs->njas', head, centre).astype(jnp.bfloat16)
    prefix = lax.optimization_barrier(prefix).astype(jnp.float32).reshape(block, BAG, D1 * D2, RANK)
    tail = jnp.take(last, wanted[:, 2, :], axis=0).astype(jnp.float32).reshape(block, BAG, RANK, D3)
    rows = jnp.einsum('njps,njsc->njpc', prefix, tail).reshape(block, BAG, D1 * D2 * D3)
    live = (jnp.arange(BAG, dtype=jnp.int32)[None, :] < counts[:, None]).astype(jnp.float32)
    return jnp.sum(rows * live[:, :, None], axis=1).astype(jnp.bfloat16)


def reference(core_ids, bag_lengths, first_core, middle_core, last_core, grad_hidden):
    block = min(BATCH, 1024)
    steps_count = BATCH // block

    def one_table(items):
        first, middle, last, wanted, counts = items
        wanted = wanted.reshape(steps_count, block, 3, BAG)
        counts = counts.reshape(steps_count, block)
        out = lax.map(lambda pair: build_rows(pair[0], pair[1], first, middle, last), (wanted, counts))
        return out.reshape(BATCH, D1 * D2 * D3)

    per_table = lax.map(one_table, (first_core, middle_core, last_core,
                                    jnp.transpose(core_ids, (1, 0, 2, 3)), jnp.transpose(bag_lengths)))
    pooled = jnp.transpose(per_table, (1, 0, 2)).reshape(BATCH, TABLES * D1 * D2 * D3)
    weight_grad = jnp.dot(pooled.T, grad_hidden, preferred_element_type=jnp.float32)
    return pooled, weight_grad
```

```python
import jax
import jax.numpy as jnp
from jax import lax
from jax.sharding import PartitionSpec as P

D1 = 8
D2 = 2
D3 = 8
RANK = 64
BAG = 2


def build_rows(wanted, first, middle, last):
    block = wanted.shape[0]
    head = jnp.take(first, wanted[:, 0, :], axis=0).reshape(block, BAG, D1, RANK)
    centre = jnp.take(middle, wanted[:, 1, :], axis=0)
    prefix = jnp.einsum("njar,njrs->njas", head, centre, preferred_element_type=jnp.float32)
    prefix = prefix.astype(jnp.bfloat16).reshape(block, BAG, D1 * D2, RANK)
    tail = jnp.take(last, wanted[:, 2, :], axis=0).reshape(block, BAG, RANK, D3)
    rows = jnp.einsum("njps,njsc->njpc", prefix, tail, preferred_element_type=jnp.float32)
    rows = rows.reshape(block, BAG, D1 * D2 * D3)
    return jnp.sum(rows, axis=1).astype(jnp.bfloat16)


def body(core_ids, bag_lengths, first_core, middle_core, last_core, grad_hidden):
    width = D1 * D2 * D3
    own, tables = bag_lengths.shape
    ncore = first_core.shape[1]
    n_data = lax.axis_size("dp")
    hidden_units = grad_hidden.shape[1]

    gathered = lax.all_gather(grad_hidden, "table", axis=0, tiled=True)

    ids = jnp.transpose(core_ids, (1, 2, 3, 0))
    lengths = jnp.transpose(bag_lengths)
    live = jnp.arange(BAG, dtype=jnp.int32)[None, :, None] < lengths[:, None, :]
    heads = jnp.where(live, ids[:, 0], ncore)
    sent = jnp.concatenate([heads, ids[:, 1], ids[:, 2]], axis=1)
    got = lax.all_to_all(sent, "table", split_axis=0, concat_axis=0, tiled=True)
    wanted = jnp.transpose(got.reshape(tables, 3, BAG, own), (0, 3, 1, 2))
    group_rows = tables * own
    block = min(group_rows, 512)
    wanted = wanted.reshape(group_rows // block, block, 3, BAG)

    first = jnp.pad(first_core[0], ((0, 8), (0, 0)))
    middle = middle_core[0]
    last = last_core[0]
    rows = lax.map(lambda w: build_rows(w, first, middle, last), wanted)
    rows = rows.reshape(group_rows, width)

    partial = lax.dot_general(
        rows, gathered, (((0,), (0,)), ((), ())), preferred_element_type=jnp.float32
    )
    partial = partial.reshape(width, n_data, hidden_units // n_data).transpose(1, 0, 2)
    weight_grad = lax.psum_scatter(partial, "dp", scatter_dimension=0, tiled=False)

    returned = lax.all_to_all(
        rows.reshape(group_rows, 1, width), "table", split_axis=0, concat_axis=1, tiled=True
    )
    pooled = returned.reshape(own, tables * width)
    return (pooled, weight_grad)


def solution(mesh):
    placed = (
        P(("dp", "table"), None, None, None),
        P(("dp", "table"), None),
        P("table", None, None),
        P("table", None, None, None),
        P("table", None, None),
        P(("dp", "table"), None),
    )
    return jax.shard_map(
        body,
        mesh=mesh,
        in_specs=placed,
        out_specs=(P(("dp", "table"), None), P("table", "dp")),
        check_vma=False,
    )
```

```python
import functools

import jax
import jax.numpy as jnp
from jax import lax
from jax.experimental import pallas as pl
from jax.experimental.pallas import tpu as pltpu
from jax.sharding import PartitionSpec as P

D1 = 8
D2 = 2
D3 = 8
RANK = 64
BAG = 2
GROUP = 16


def rows_kernel(ids_ref, first_ref, middle_ref, last_ref, out_ref):
    f32 = jnp.float32
    bf16 = jnp.bfloat16
    own = out_ref.shape[0]
    row16 = lax.broadcasted_iota(jnp.int32, (16, 128), 0)
    lane16 = lax.broadcasted_iota(jnp.int32, (16, 128), 1)
    keep = ((row16 < 8) == (lane16 < 64)).astype(bf16)
    zero = jnp.zeros((16, 128), bf16)
    block = lax.broadcasted_iota(jnp.int32, (8, 128), 1) // 16
    sub = lax.broadcasted_iota(jnp.int32, (8, 128), 0)

    def group(g, carry):
        base = g * GROUP
        prefixes, tails = [], [[], []]
        for k in range(0, GROUP, 2):
            heads, centres = [], []
            for j in range(BAG):
                n0, n1 = base + k, base + k + 1
                pair = [first_ref[ids_ref[j, n0]], first_ref[ids_ref[j, n1]]]
                heads.append(jnp.concatenate(pair, axis=0).astype(bf16) * keep)
                centres += [middle_ref[ids_ref[2 + j, n0]], middle_ref[ids_ref[2 + j, n1]]]
                tails[j] += [last_ref[ids_ref[4 + j, n0]], last_ref[ids_ref[4 + j, n1]]]
            left = jnp.concatenate(
                [
                    jnp.concatenate([heads[0], zero], axis=1),
                    jnp.concatenate([zero, heads[1]], axis=1),
                ],
                axis=0,
            )
            product = jnp.dot(left, jnp.concatenate(centres, axis=0), preferred_element_type=f32)
            prefixes.append(jnp.concatenate([product[:16], product[16:]], axis=1).astype(bf16))
        prefix = jnp.concatenate(prefixes, axis=0)
        tail = jnp.concatenate([jnp.concatenate(t, axis=0) for t in tails], axis=1)
        product = lax.dot_general(prefix, tail, (((1,), (1,)), ((), ())), preferred_element_type=f32)
        finished = []
        for h in range(GROUP // 8):
            part = product[h * 64 : h * 64 + 64, h * 128 : h * 128 + 128]
            mixed = part[:8]
            for n in range(1, 8):
                mixed = jnp.where(block == n, part[n * 8 : n * 8 + 8], mixed)
            for k in (1, 2, 4):
                up = pltpu.roll(pltpu.roll(mixed, 8 - k, 0), 16 * k, 1)
                down = pltpu.roll(pltpu.roll(mixed, k, 0), 128 - 16 * k, 1)
                high = (block & k) != 0
                same = ((sub & k) != 0) == high
                mixed = jnp.where(same, mixed, jnp.where(high, up, down))
            finished.append(mixed)
        row = pl.multiple_of(base, GROUP)
        out_ref[pl.ds(row, GROUP), :] = jnp.concatenate(finished, axis=0).astype(bf16)
        return carry

    lax.fori_loop(0, own // GROUP, group, 0, unroll=True)


def table_rows(got, first, middle, last):
    senders, words, own = got.shape
    ncore = first.shape[0]
    width = D1 * D2 * D3
    head = first.reshape(ncore, D1, RANK).astype(jnp.float32)
    head = jnp.pad(jnp.concatenate([head, head], axis=2), ((0, 8), (0, 0), (0, 0)))
    tail = last.reshape(ncore, RANK, D3).transpose(0, 2, 1)
    blank = jnp.zeros_like(tail)
    tail = jnp.concatenate(
        [jnp.concatenate([tail, blank], axis=2), jnp.concatenate([blank, tail], axis=2)], axis=1
    )

    def whole(x):
        return pl.BlockSpec(x.shape, lambda i: (0,) * x.ndim, pipeline_mode=pl.Buffered(1))

    lookups = senders * own * BAG
    return pl.pallas_call(
        rows_kernel,
        out_shape=jax.ShapeDtypeStruct((senders, own, width), jnp.bfloat16),
        grid=(senders,),
        in_specs=[
            pl.BlockSpec((None, words, own), lambda i: (i, 0, 0), memory_space=pltpu.SMEM),
            whole(head),
            whole(middle),
            whole(tail),
        ],
        out_specs=pl.BlockSpec((None, own, width), lambda i: (i, 0, 0)),
        compiler_params=pltpu.CompilerParams(vmem_limit_bytes=48 << 20),
        cost_estimate=pl.CostEstimate(
            flops=lookups * 4096 * 128, bytes_accessed=8 << 20, transcendentals=0
        ),
    )(got, head, middle, tail)


def product_kernel(rows_ref, grad_ref, out_ref):
    @pl.when(pl.program_id(0) == 0)
    def _():
        out_ref[...] = jnp.zeros_like(out_ref)

    parts, _, columns = out_ref.shape
    rows = rows_ref[...]
    for d in range(parts):
        out_ref[d] += lax.dot_general(
            rows,
            grad_ref[:, d * columns : (d + 1) * columns],
            (((0,), (0,)), ((), ())),
            preferred_element_type=jnp.float32,
        )


def partial_product(rows, grad, parts):
    samples, width = rows.shape
    hidden_units = grad.shape[1]
    step = min(samples, 512)
    shape = (parts, width, hidden_units // parts)
    return pl.pallas_call(
        product_kernel,
        out_shape=jax.ShapeDtypeStruct(shape, jnp.float32),
        grid=(samples // step,),
        in_specs=[
            pl.BlockSpec((step, width), lambda i: (i, 0)),
            pl.BlockSpec((step, hidden_units), lambda i: (i, 0)),
        ],
        out_specs=pl.BlockSpec(shape, lambda i: (0, 0, 0)),
        cost_estimate=pl.CostEstimate(
            flops=2 * samples * width * hidden_units,
            bytes_accessed=2 * samples * (width + hidden_units),
            transcendentals=0,
        ),
    )(rows, grad)


def body(core_ids, bag_lengths, first_core, middle_core, last_core, grad_hidden):
    width = D1 * D2 * D3
    own, tables = bag_lengths.shape
    ncore = first_core.shape[1]
    n_data = lax.axis_size("dp")

    gathered = lax.all_gather(grad_hidden, "table", axis=0, tiled=True)

    ids = jnp.transpose(core_ids, (1, 2, 3, 0))
    lengths = jnp.transpose(bag_lengths)
    live = jnp.arange(BAG, dtype=jnp.int32)[None, :, None] < lengths[:, None, :]
    heads = jnp.where(live, ids[:, 0], ncore)
    sent = jnp.concatenate([heads, ids[:, 1], ids[:, 2]], axis=1)
    got = lax.all_to_all(sent, "table", split_axis=0, concat_axis=0, tiled=True)

    rows = table_rows(got, first_core[0], middle_core[0], last_core[0])

    partial = partial_product(rows.reshape(tables * own, width), gathered, n_data)
    weight_grad = lax.psum_scatter(partial, "dp", scatter_dimension=0, tiled=False)

    returned = lax.all_to_all(rows, "table", split_axis=0, concat_axis=0, tiled=True)
    pooled = jnp.transpose(returned, (1, 0, 2)).reshape(own, tables * width)
    return (pooled, weight_grad)


def solution(mesh):
    placed = (
        P(("dp", "table"), None, None, None),
        P(("dp", "table"), None),
        P("table", None, None),
        P("table", None, None, None),
        P("table", None, None),
        P(("dp", "table"), None),
    )
    return jax.shard_map(
        body,
        mesh=mesh,
        in_specs=placed,
        out_specs=(P(("dp", "table"), None), P("table", "dp")),
        check_vma=False,
    )
```

```python
import functools

import jax
import jax.numpy as jnp
from jax import lax
from jax.experimental import pallas as pl
from jax.experimental.pallas import tpu as pltpu
from jax.sharding import Mesh
from jax.sharding import PartitionSpec as P

D1 = 8
D2 = 2
D3 = 8
RANK = 64
BAG = 2
WIDTH = D1 * D2 * D3
BLOCK = 128
SPLIT = (64, 32, 32)
NX = 4
NY = 4
NCORES = 2
TABLE = ("x", "y", "core")
EVERY = ("dp", "x", "y", "core")


def rows_kernel(ids_ref, first_ref, middle_ref, last_ref, out_ref, prefix_ref, mixed_ref, *, offset):
    f32 = jnp.float32
    bf16 = jnp.bfloat16
    senders, part, _ = out_ref.shape
    per_block = BLOCK // part
    blocks = senders // per_block
    groups = BLOCK // 8
    row16 = lax.broadcasted_iota(jnp.int32, (16, 128), 0)
    lane16 = lax.broadcasted_iota(jnp.int32, (16, 128), 1)
    keep = ((row16 < 8) == (lane16 < 64)).astype(bf16)
    zero = jnp.zeros((16, 128), bf16)
    lane = lax.broadcasted_iota(jnp.int32, (8, 128), 1) // 16

    def index(i, word, sample):
        return ids_ref[i * per_block + sample // part, word, offset + sample % part]

    def prefixes(i, g):
        for n in range(0, 8, 2):
            pair = (n * groups + g, (n + 1) * groups + g)
            heads, centres = [], []
            for j in range(BAG):
                two = [first_ref[index(i, j, a)] for a in pair]
                heads.append(jnp.concatenate(two, axis=0).astype(bf16) * keep)
                centres += [middle_ref[index(i, 2 + j, a)] for a in pair]
            left = jnp.concatenate(
                [
                    jnp.concatenate([heads[0], zero], axis=1),
                    jnp.concatenate([zero, heads[1]], axis=1),
                ],
                axis=0,
            )
            product = jnp.dot(left, jnp.concatenate(centres, axis=0), preferred_element_type=f32)
            product = product.astype(bf16)
            at = g * 64 + n * 8
            prefix_ref[at : at + 16, :128] = product[:16]
            prefix_ref[at : at + 16, 128:] = product[16:]

    def contract(i, g):
        tails = [
            jnp.concatenate(
                [last_ref[index(i, 4 + j, n * groups + e)] for e in (g, g + 1) for n in range(8)],
                axis=0,
            )
            for j in range(BAG)
        ]
        product = lax.dot_general(
            prefix_ref[g * 64 : g * 64 + 128, :],
            jnp.concatenate(tails, axis=1),
            (((1,), (1,)), ((), ())),
            preferred_element_type=f32,
        )
        for e in range(2):
            own = product[e * 64 : e * 64 + 64, e * 128 : e * 128 + 128]
            mixed = own[:8]
            for n in range(1, 8):
                mixed = jnp.where(lane == n, own[n * 8 : n * 8 + 8], mixed)
            mixed_ref[(g + e) * 8 : (g + e) * 8 + 8, :] = mixed

    def arrange(i, h):
        parts = [mixed_ref[pl.ds(h * 8 + a, 8, stride=8), :] for a in range(8)]
        for k in (1, 2, 4):
            low = (lane & k) == 0
            moved = list(parts)
            for a in range(8):
                if a & k == 0:
                    p, q = parts[a], parts[a + k]
                    moved[a] = jnp.where(low, p, pltpu.roll(q, 16 * k, 1))
                    moved[a + k] = jnp.where(low, pltpu.roll(p, 128 - 16 * k, 1), q)
            parts = moved
        for n in range(8):
            at = n * groups + h
            out_ref[i * per_block + at // part, at % part : at % part + 8, :] = parts[n].astype(bf16)

    def step(i, carry):
        now = jnp.minimum(i, blocks - 1)
        before = jnp.clip(i - 1, 0, blocks - 1)
        earlier = jnp.clip(i - 2, 0, blocks - 1)
        for h in range(0, groups, 8):
            arrange(earlier, h)
        for g in range(0, groups, 2):
            contract(before, g)
            prefixes(now, g)
            prefixes(now, g + 1)
        return carry

    lax.fori_loop(0, blocks + 2, step, 0)


def table_rows(got, head, middle, tail, offset, part):
    senders = got.shape[0]
    lookups = senders * part * BAG
    vmem = pl.BlockSpec(memory_space=pltpu.VMEM)
    return pl.pallas_call(
        functools.partial(rows_kernel, offset=offset),
        out_shape=jax.ShapeDtypeStruct((senders, part, WIDTH), jnp.bfloat16),
        in_specs=[pl.BlockSpec(memory_space=pltpu.SMEM), vmem, vmem, vmem],
        out_specs=vmem,
        scratch_shapes=[
            pltpu.VMEM((BLOCK * 8, 256), jnp.bfloat16),
            pltpu.VMEM((BLOCK, 128), jnp.float32),
        ],
        compiler_params=pltpu.CompilerParams(vmem_limit_bytes=32 << 20),
        cost_estimate=pl.CostEstimate(
            flops=lookups * 2000000, bytes_accessed=6 << 20, transcendentals=0
        ),
    )(got, head, middle, tail)


def product_kernel(place_ref, *refs):
    rows_refs = refs[: len(SPLIT)]
    left_refs = refs[len(SPLIT) : len(SPLIT) + NCORES * NY]
    right_refs = refs[len(SPLIT) + NCORES * NY : len(SPLIT) + NCORES * (NX + NY)]
    own_ref, out_refs, total_ref = refs[-5], refs[-4:-1], refs[-1]
    me, x, y, core = place_ref[0], place_ref[1], place_ref[2], place_ref[3]
    half = left_refs[0].shape[2]

    def rows_from(sx, sy, sc):
        sender = (sx * NY + sy) * NCORES + sc
        return [ref[sender] for ref in rows_refs]

    def add(value, first, columns):
        if first:
            total_ref[:, columns] = value
        else:
            total_ref[:, columns] += value

    for c in range(NCORES):
        sc = (core + c) % NCORES
        for m in range(NY):
            for refs_of, columns, turn in (
                (left_refs, slice(0, half), False),
                (right_refs, slice(half, 2 * half), True),
            ):
                rows = []
                for k in range(NX):
                    a, b = (m, k) if turn else (k, m)
                    rows += rows_from((x - a + NX) % NX, (y - b + NY) % NY, sc)
                rows = jnp.concatenate(rows, axis=0)
                grad = refs_of[c * NY + m][...]
                grad = grad.reshape(grad.shape[0] * grad.shape[1], half)
                value = lax.dot_general(
                    rows, grad, (((0,), (0,)), ((), ())), preferred_element_type=jnp.float32
                )
                add(value, c == 0 and m == 0, columns)

    columns = own_ref.shape[1]

    def block(k):
        at = pl.multiple_of(((me + k) % 4) * columns, columns)
        return total_ref[:, pl.ds(at, columns)]

    own_ref[...] = block(0)
    for k in range(3):
        out_refs[k][...] = block(k + 1).astype(jnp.bfloat16)


def partial_product(rows, left, right, place):
    senders = rows[0].shape[0]
    columns = 2 * left[0].shape[2]
    quarter = columns // 4
    samples = senders * sum(SPLIT)
    vmem = pl.BlockSpec(memory_space=pltpu.VMEM)
    operands = [*rows, *left, *right]
    return pl.pallas_call(
        product_kernel,
        out_shape=[jax.ShapeDtypeStruct((WIDTH, quarter), jnp.float32)]
        + [jax.ShapeDtypeStruct((WIDTH, quarter), jnp.bfloat16)] * 3,
        in_specs=[pl.BlockSpec(memory_space=pltpu.SMEM)] + [vmem] * len(operands),
        out_specs=[vmem] * 4,
        scratch_shapes=[pltpu.VMEM((WIDTH, columns), jnp.float32)],
        compiler_params=pltpu.CompilerParams(vmem_limit_bytes=32 << 20),
        cost_estimate=pl.CostEstimate(
            flops=2 * samples * WIDTH * columns,
            bytes_accessed=2 * samples * (WIDTH + columns),
            transcendentals=0,
        ),
    )(place, *operands)


def around(axis, size, value):
    out = [value]
    for k in range(1, size):
        out.append(lax.ppermute(value, axis, [(i, (i + k) % size) for i in range(size)]))
    return out


def body(core_ids, bag_lengths, first_core, middle_core, last_core, grad_hidden):
    own, tables = bag_lengths.shape
    ncore = first_core.shape[1]
    half = grad_hidden.shape[1] // 2
    swap = [(0, 1), (1, 0)]

    left = around("x", NX, grad_hidden[:, :half])
    right = around("y", NY, grad_hidden[:, half:])

    ids = jnp.transpose(core_ids, (1, 2, 3, 0))
    lengths = jnp.transpose(bag_lengths)
    live = jnp.arange(BAG, dtype=jnp.int32)[None, :, None] < lengths[:, None, :]
    heads = jnp.where(live, ids[:, 0], ncore)
    sent = jnp.concatenate([heads, ids[:, 1], ids[:, 2]], axis=1)
    got = lax.all_to_all(sent, TABLE, split_axis=0, concat_axis=0, tiled=True)

    middle = middle_core[0]
    head = first_core[0].reshape(ncore, D1, RANK).astype(jnp.float32)
    head = jnp.pad(jnp.concatenate([head, head], axis=2), ((0, 8), (0, 0), (0, 0)))
    tail = last_core[0].reshape(ncore, RANK, D3).transpose(0, 2, 1)
    blank = jnp.zeros_like(tail)
    tail = jnp.concatenate(
        [jnp.concatenate([tail, blank], axis=2), jnp.concatenate([blank, tail], axis=2)], axis=1
    )

    left, right = jnp.stack(left), jnp.stack(right)
    got, left, right = lax.optimization_barrier((got, left, right))
    left = around("y", NY, left)
    right = around("x", NX, right)

    rows, returned = [], []
    offset = 0
    for number, part in enumerate(SPLIT):
        if number == len(SPLIT) - 1:
            got, left, right = lax.optimization_barrier((got, left, right))
            left = left + [lax.ppermute(v, "core", swap) for v in left]
            right = right + [lax.ppermute(v, "core", swap) for v in right]
        rows.append(table_rows(got, head, middle, tail, offset, part))
        returned.append(lax.all_to_all(rows[-1], TABLE, split_axis=0, concat_axis=0, tiled=True))
        offset += part

    me = lax.axis_index("dp")
    place = jnp.stack([me, lax.axis_index("x"), lax.axis_index("y"), lax.axis_index("core")])
    mine, *others = partial_product(rows, left, right, place.astype(jnp.int32))
    weight_grad = mine
    for k, other in enumerate(others):
        came = lax.ppermute(other, "dp", [(i, (i + k + 1) % 4) for i in range(4)])
        weight_grad = weight_grad + came.astype(jnp.float32)

    pooled = jnp.concatenate(
        [jnp.transpose(r, (1, 0, 2)).reshape(r.shape[1], tables * WIDTH) for r in returned], axis=0
    )
    return (pooled, weight_grad)


def solution(mesh):
    n_data = mesh.devices.shape[0]
    fine = Mesh(mesh.devices.reshape(n_data, NX, NY, NCORES), EVERY)
    placed = (
        P(EVERY, None, None, None),
        P(EVERY, None),
        P(TABLE, None, None),
        P(TABLE, None, None, None),
        P(TABLE, None, None),
        P(EVERY, None),
    )
    return jax.shard_map(
        body,
        mesh=fine,
        in_specs=placed,
        out_specs=(P(EVERY, None), P(TABLE, "dp")),
        check_vma=False,
    )
```

```python
import jax
import jax.numpy as jnp
from jax import lax
from jax.experimental import pallas as pl
from jax.experimental.pallas import tpu as pltpu
from jax.sharding import PartitionSpec as P

D1 = 8
D2 = 2
D3 = 8
RANK = 64
BAG = 2
WIDTH = D1 * D2 * D3
BLOCK = 128


def rows_kernel(ids_ref, first_ref, middle_ref, last_ref, out_ref, prefix_ref, mixed_ref):
    f32 = jnp.float32
    bf16 = jnp.bfloat16
    senders, part, _ = out_ref.shape
    per_block = BLOCK // part
    blocks = senders // per_block
    groups = BLOCK // 8
    row16 = lax.broadcasted_iota(jnp.int32, (16, 128), 0)
    lane16 = lax.broadcasted_iota(jnp.int32, (16, 128), 1)
    keep = ((row16 < 8) == (lane16 < 64)).astype(bf16)
    zero = jnp.zeros((16, 128), bf16)
    lane = lax.broadcasted_iota(jnp.int32, (8, 128), 1) // 16

    def index(i, word, sample):
        return ids_ref[i * per_block + sample // part, word, sample % part]

    def prefixes(i, g):
        for n in range(0, 8, 2):
            pair = (n * groups + g, (n + 1) * groups + g)
            heads, centres = [], []
            for j in range(BAG):
                two = [first_ref[index(i, j, a)] for a in pair]
                heads.append(jnp.concatenate(two, axis=0).astype(bf16) * keep)
                centres += [middle_ref[index(i, 2 + j, a)] for a in pair]
            left = jnp.concatenate(
                [
                    jnp.concatenate([heads[0], zero], axis=1),
                    jnp.concatenate([zero, heads[1]], axis=1),
                ],
                axis=0,
            )
            product = jnp.dot(left, jnp.concatenate(centres, axis=0), preferred_element_type=f32)
            product = product.astype(bf16)
            at = g * 64 + n * 8
            prefix_ref[at : at + 16, :128] = product[:16]
            prefix_ref[at : at + 16, 128:] = product[16:]

    def contract(i, g):
        tails = [
            jnp.concatenate(
                [last_ref[index(i, 4 + j, n * groups + e)] for e in (g, g + 1) for n in range(8)],
                axis=0,
            )
            for j in range(BAG)
        ]
        product = lax.dot_general(
            prefix_ref[g * 64 : g * 64 + 128, :],
            jnp.concatenate(tails, axis=1),
            (((1,), (1,)), ((), ())),
            preferred_element_type=f32,
        )
        for e in range(2):
            own = product[e * 64 : e * 64 + 64, e * 128 : e * 128 + 128]
            mixed = own[:8]
            for n in range(1, 8):
                mixed = jnp.where(lane == n, own[n * 8 : n * 8 + 8], mixed)
            mixed_ref[(g + e) * 8 : (g + e) * 8 + 8, :] = mixed

    def arrange(i, h):
        parts = [mixed_ref[pl.ds(h * 8 + a, 8, stride=8), :] for a in range(8)]
        for k in (1, 2, 4):
            low = (lane & k) == 0
            moved = list(parts)
            for a in range(8):
                if a & k == 0:
                    p, q = parts[a], parts[a + k]
                    moved[a] = jnp.where(low, p, pltpu.roll(q, 16 * k, 1))
                    moved[a + k] = jnp.where(low, pltpu.roll(p, 128 - 16 * k, 1), q)
            parts = moved
        for n in range(8):
            at = n * groups + h
            out_ref[i * per_block + at // part, at % part : at % part + 8, :] = parts[n].astype(bf16)

    def step(i, carry):
        now = jnp.minimum(i, blocks - 1)
        before = jnp.clip(i - 1, 0, blocks - 1)
        earlier = jnp.clip(i - 2, 0, blocks - 1)
        for h in range(0, groups, 8):
            arrange(earlier, h)
        for g in range(0, groups, 2):
            contract(before, g)
            prefixes(now, g)
            prefixes(now, g + 1)
        return carry

    lax.fori_loop(0, blocks + 2, step, 0)


def table_rows(got, head, middle, tail):
    senders, _, own = got.shape
    lookups = senders * own * BAG
    vmem = pl.BlockSpec(memory_space=pltpu.VMEM)
    return pl.pallas_call(
        rows_kernel,
        out_shape=jax.ShapeDtypeStruct((senders, own, WIDTH), jnp.bfloat16),
        in_specs=[pl.BlockSpec(memory_space=pltpu.SMEM), vmem, vmem, vmem],
        out_specs=vmem,
        scratch_shapes=[
            pltpu.VMEM((BLOCK * 8, 256), jnp.bfloat16),
            pltpu.VMEM((BLOCK, 128), jnp.float32),
        ],
        compiler_params=pltpu.CompilerParams(vmem_limit_bytes=32 << 20),
        cost_estimate=pl.CostEstimate(
            flops=lookups * 2000000, bytes_accessed=6 << 20, transcendentals=0
        ),
    )(got, head, middle, tail)


def product_kernel(rows_ref, grad_ref, out_ref, total_ref):
    step = pl.program_id(0)
    value = lax.dot_general(
        rows_ref[...], grad_ref[...], (((0,), (0,)), ((), ())), preferred_element_type=jnp.float32
    )

    @pl.when(step == 0)
    def _():
        total_ref[...] = value

    @pl.when(step > 0)
    def _():
        total_ref[...] += value

    @pl.when(step == pl.num_programs(0) - 1)
    def _():
        parts, _, columns = out_ref.shape
        for d in range(parts):
            out_ref[d] = total_ref[:, d * columns : (d + 1) * columns]


def partial_product(rows, grad, parts):
    samples, width = rows.shape
    hidden_units = grad.shape[1]
    step = min(samples, 512)
    shape = (parts, width, hidden_units // parts)
    return pl.pallas_call(
        product_kernel,
        out_shape=jax.ShapeDtypeStruct(shape, jnp.float32),
        grid=(samples // step,),
        in_specs=[
            pl.BlockSpec((step, width), lambda i: (i, 0)),
            pl.BlockSpec((step, hidden_units), lambda i: (i, 0)),
        ],
        out_specs=pl.BlockSpec(shape, lambda i: (0, 0, 0)),
        scratch_shapes=[pltpu.VMEM((width, hidden_units), jnp.float32)],
        cost_estimate=pl.CostEstimate(
            flops=2 * samples * width * hidden_units,
            bytes_accessed=2 * samples * (width + hidden_units),
            transcendentals=0,
        ),
    )(rows, grad)


def body(core_ids, bag_lengths, first_core, middle_core, last_core, grad_hidden):
    own, tables = bag_lengths.shape
    ncore = first_core.shape[1]
    n_data = lax.axis_size("dp")

    gathered = lax.all_gather(grad_hidden, "table", axis=0, tiled=True)

    ids = jnp.transpose(core_ids, (1, 2, 3, 0))
    lengths = jnp.transpose(bag_lengths)
    live = jnp.arange(BAG, dtype=jnp.int32)[None, :, None] < lengths[:, None, :]
    heads = jnp.where(live, ids[:, 0], ncore)
    sent = jnp.concatenate([heads, ids[:, 1], ids[:, 2]], axis=1)
    got = lax.all_to_all(sent, "table", split_axis=0, concat_axis=0, tiled=True)

    head = first_core[0].reshape(ncore, D1, RANK).astype(jnp.float32)
    head = jnp.pad(jnp.concatenate([head, head], axis=2), ((0, 8), (0, 0), (0, 0)))
    tail = last_core[0].reshape(ncore, RANK, D3).transpose(0, 2, 1)
    blank = jnp.zeros_like(tail)
    tail = jnp.concatenate(
        [jnp.concatenate([tail, blank], axis=2), jnp.concatenate([blank, tail], axis=2)], axis=1
    )
    rows = table_rows(got, head, middle_core[0], tail)

    partial = partial_product(rows.reshape(tables * own, WIDTH), gathered, n_data)
    weight_grad = lax.psum_scatter(partial, "dp", scatter_dimension=0, tiled=False)

    returned = lax.all_to_all(rows, "table", split_axis=0, concat_axis=0, tiled=True)
    pooled = jnp.transpose(returned, (1, 0, 2)).reshape(own, tables * WIDTH)
    return (pooled, weight_grad)


def solution(mesh):
    placed = (
        P(("dp", "table"), None, None, None),
        P(("dp", "table"), None),
        P("table", None, None),
        P("table", None, None, None),
        P("table", None, None),
        P(("dp", "table"), None),
    )
    return jax.shard_map(
        body,
        mesh=mesh,
        in_specs=placed,
        out_specs=(P(("dp", "table"), None), P("table", "dp")),
        check_vma=False,
    )
```

```python
import jax
import jax.numpy as jnp
from jax import lax
from jax.experimental import pallas as pl
from jax.experimental.pallas import tpu as pltpu
from jax.sharding import PartitionSpec as P

D1 = 8
D2 = 2
D3 = 8
RANK = 64
BAG = 2
WIDTH = D1 * D2 * D3
BLOCK = 128


def rows_kernel(ids_ref, first_ref, middle_ref, last_ref, out_ref, prefix_ref, mixed_ref):
    f32 = jnp.float32
    bf16 = jnp.bfloat16
    senders, part, _ = out_ref.shape
    per_block = BLOCK // part
    blocks = senders // per_block
    groups = BLOCK // 8
    row16 = lax.broadcasted_iota(jnp.int32, (16, 128), 0)
    lane16 = lax.broadcasted_iota(jnp.int32, (16, 128), 1)
    keep = ((row16 < 8) == (lane16 < 64)).astype(bf16)
    zero = jnp.zeros((16, 128), bf16)
    lane = lax.broadcasted_iota(jnp.int32, (8, 128), 1) // 16

    def index(i, word, sample):
        return ids_ref[i * per_block + sample // part, word // BAG, word % BAG, sample % part]

    def prefixes(i, g):
        for n in range(0, 8, 2):
            pair = (n * groups + g, (n + 1) * groups + g)
            heads, centres = [], []
            for j in range(BAG):
                two = [first_ref[index(i, j, a)] for a in pair]
                heads.append(jnp.concatenate(two, axis=0).astype(bf16) * keep)
                centres += [middle_ref[index(i, 2 + j, a)] for a in pair]
            left = jnp.concatenate(
                [
                    jnp.concatenate([heads[0], zero], axis=1),
                    jnp.concatenate([zero, heads[1]], axis=1),
                ],
                axis=0,
            )
            product = jnp.dot(left, jnp.concatenate(centres, axis=0), preferred_element_type=f32)
            product = product.astype(bf16)
            at = g * 64 + n * 8
            prefix_ref[at : at + 16, :128] = product[:16]
            prefix_ref[at : at + 16, 128:] = product[16:]

    def contract(i, g):
        tails = [
            jnp.concatenate(
                [last_ref[index(i, 4 + j, n * groups + e)] for e in (g, g + 1) for n in range(8)],
                axis=0,
            )
            for j in range(BAG)
        ]
        product = lax.dot_general(
            prefix_ref[g * 64 : g * 64 + 128, :],
            jnp.concatenate(tails, axis=1),
            (((1,), (1,)), ((), ())),
            preferred_element_type=f32,
        )
        for e in range(2):
            own = product[e * 64 : e * 64 + 64, e * 128 : e * 128 + 128]
            mixed = own[:8]
            for n in range(1, 8):
                mixed = jnp.where(lane == n, own[n * 8 : n * 8 + 8], mixed)
            mixed_ref[(g + e) * 8 : (g + e) * 8 + 8, :] = mixed

    def arrange(i, h):
        parts = [mixed_ref[pl.ds(h * 8 + a, 8, stride=8), :] for a in range(8)]
        for k in (1, 2, 4):
            low = (lane & k) == 0
            moved = list(parts)
            for a in range(8):
                if a & k == 0:
                    p, q = parts[a], parts[a + k]
                    moved[a] = jnp.where(low, p, pltpu.roll(q, 16 * k, 1))
                    moved[a + k] = jnp.where(low, pltpu.roll(p, 128 - 16 * k, 1), q)
            parts = moved
        for n in range(8):
            at = n * groups + h
            out_ref[i * per_block + at // part, at % part : at % part + 8, :] = parts[n].astype(bf16)

    def step(i, carry):
        now = jnp.minimum(i, blocks - 1)
        before = jnp.clip(i - 1, 0, blocks - 1)
        earlier = jnp.clip(i - 2, 0, blocks - 1)
        for h in range(0, groups, 8):
            arrange(earlier, h)
        for g in range(0, groups, 2):
            contract(before, g)
            prefixes(now, g)
            prefixes(now, g + 1)
        return carry

    lax.fori_loop(0, blocks + 2, step, 0)


def table_rows(got, head, middle, tail):
    senders, own = got.shape[0], got.shape[-1]
    lookups = senders * own * BAG
    vmem = pl.BlockSpec(memory_space=pltpu.VMEM)
    return pl.pallas_call(
        rows_kernel,
        out_shape=jax.ShapeDtypeStruct((senders, own, WIDTH), jnp.bfloat16),
        in_specs=[pl.BlockSpec(memory_space=pltpu.SMEM), vmem, vmem, vmem],
        out_specs=vmem,
        scratch_shapes=[
            pltpu.VMEM((BLOCK * 8, 256), jnp.bfloat16),
            pltpu.VMEM((BLOCK, 128), jnp.float32),
        ],
        compiler_params=pltpu.CompilerParams(vmem_limit_bytes=32 << 20),
        cost_estimate=pl.CostEstimate(
            flops=lookups * 2000000, bytes_accessed=6 << 20, transcendentals=0
        ),
    )(got, head, middle, tail)


def product_kernel(rows_ref, grad_ref, out_ref, held_ref, total_ref, sems):
    chunks, size, _ = held_ref.shape
    copies = []
    for i in range(chunks):
        source = grad_ref.at[pl.ds(i * size, size)]
        copies.append(pltpu.make_async_copy(source, held_ref.at[i], sems.at[i]))
        copies[-1].start()
    for i in range(chunks):
        copies[i].wait()
        value = lax.dot_general(
            rows_ref[i * size : (i + 1) * size, :],
            held_ref[i],
            (((0,), (0,)), ((), ())),
            preferred_element_type=jnp.float32,
        )
        if i == 0:
            total_ref[...] = value
        elif i < chunks - 1:
            total_ref[...] += value
        else:
            value += total_ref[...]
            parts, _, columns = out_ref.shape
            for d in range(parts):
                out_ref[d] = value[:, d * columns : (d + 1) * columns]


def partial_product(rows, grad, parts):
    samples, width = rows.shape
    hidden_units = grad.shape[1]
    size = min(samples, 512)
    vmem = pl.BlockSpec(memory_space=pltpu.VMEM)
    return pl.pallas_call(
        product_kernel,
        out_shape=jax.ShapeDtypeStruct((parts, width, hidden_units // parts), jnp.float32),
        in_specs=[vmem, pl.BlockSpec(memory_space=pltpu.HBM)],
        out_specs=vmem,
        scratch_shapes=[
            pltpu.VMEM((samples // size, size, hidden_units), grad.dtype),
            pltpu.VMEM((width, hidden_units), jnp.float32),
            pltpu.SemaphoreType.DMA((samples // size,)),
        ],
        compiler_params=pltpu.CompilerParams(vmem_limit_bytes=54 << 20),
        cost_estimate=pl.CostEstimate(
            flops=2 * samples * width * hidden_units,
            bytes_accessed=2 * samples * (width + hidden_units),
            transcendentals=0,
        ),
    )(rows, grad)


def beside_kernel(blocks_ref, out_ref):
    tables, _, width = blocks_ref.shape
    for t in range(tables):
        out_ref[:, t * width : (t + 1) * width] = blocks_ref[t]


def side_by_side(blocks):
    tables, own, width = blocks.shape
    step = min(own, 32)
    return pl.pallas_call(
        beside_kernel,
        out_shape=jax.ShapeDtypeStruct((own, tables * width), blocks.dtype),
        grid=(own // step,),
        in_specs=[pl.BlockSpec((tables, step, width), lambda i: (0, i, 0))],
        out_specs=pl.BlockSpec((step, tables * width), lambda i: (i, 0)),
    )(blocks)


def body(core_ids, bag_lengths, first_core, middle_core, last_core, grad_hidden):
    own, tables = bag_lengths.shape
    ncore = first_core.shape[1]
    n_data = lax.axis_size("dp")

    gathered = lax.all_gather(grad_hidden, "table", axis=0, tiled=True)

    ids = jnp.transpose(core_ids, (1, 2, 3, 0))
    lengths = jnp.transpose(bag_lengths)[:, None, None, :]
    core = lax.broadcasted_iota(jnp.int32, ids.shape, 1)
    slot = lax.broadcasted_iota(jnp.int32, ids.shape, 2)
    sent = jnp.where((core == 0) & (slot >= lengths), ncore, ids)
    got = lax.all_to_all(sent, "table", split_axis=0, concat_axis=0, tiled=True)

    head = first_core[0].reshape(ncore, D1, RANK).astype(jnp.float32)
    head = jnp.pad(jnp.concatenate([head, head], axis=2), ((0, 8), (0, 0), (0, 0)))
    tail = last_core[0].reshape(ncore, RANK, D3).transpose(0, 2, 1)
    blank = jnp.zeros_like(tail)
    tail = jnp.concatenate(
        [jnp.concatenate([tail, blank], axis=2), jnp.concatenate([blank, tail], axis=2)], axis=1
    )
    rows = table_rows(got, head, middle_core[0], tail)

    partial = partial_product(rows.reshape(tables * own, WIDTH), gathered, n_data)
    weight_grad = lax.psum_scatter(partial, "dp", scatter_dimension=0, tiled=False)

    returned = lax.all_to_all(rows, "table", split_axis=0, concat_axis=0, tiled=True)
    pooled = side_by_side(returned)
    return (pooled, weight_grad)


def solution(mesh):
    placed = (
        P(("dp", "table"), None, None, None),
        P(("dp", "table"), None),
        P("table", None, None),
        P("table", None, None, None),
        P("table", None, None),
        P(("dp", "table"), None),
    )
    return jax.shard_map(
        body,
        mesh=mesh,
        in_specs=placed,
        out_specs=(P(("dp", "table"), None), P("table", "dp")),
        check_vma=False,
    )
```

```python
import jax
import jax.numpy as jnp
from jax import lax
from jax.experimental import pallas as pl
from jax.experimental.pallas import tpu as pltpu
from jax.sharding import PartitionSpec as P

D1 = 8
D2 = 2
D3 = 8
RANK = 64
BAG = 2
WIDTH = D1 * D2 * D3
BLOCK = 128


def rows_kernel(ids_ref, first_ref, middle_ref, last_ref, out_ref, prefix_ref, mixed_ref):
    f32 = jnp.float32
    bf16 = jnp.bfloat16
    senders, part, _ = out_ref.shape
    per_block = BLOCK // part
    blocks = senders // per_block
    groups = BLOCK // 8
    row16 = lax.broadcasted_iota(jnp.int32, (16, 128), 0)
    lane16 = lax.broadcasted_iota(jnp.int32, (16, 128), 1)
    keep = ((row16 < 8) == (lane16 < 64)).astype(bf16)
    zero = jnp.zeros((16, 128), bf16)
    lane = lax.broadcasted_iota(jnp.int32, (8, 128), 1) // 16

    def index(i, word, sample):
        return ids_ref[i * per_block + sample // part, word // BAG, word % BAG, sample % part]

    def prefixes(i, g):
        for n in range(0, 8, 2):
            pair = (n * groups + g, (n + 1) * groups + g)
            heads, centres = [], []
            for j in range(BAG):
                two = [first_ref[index(i, j, a)] for a in pair]
                heads.append(jnp.concatenate(two, axis=0).astype(bf16) * keep)
                centres += [middle_ref[index(i, 2 + j, a)] for a in pair]
            left = jnp.concatenate(
                [
                    jnp.concatenate([heads[0], zero], axis=1),
                    jnp.concatenate([zero, heads[1]], axis=1),
                ],
                axis=0,
            )
            product = jnp.dot(left, jnp.concatenate(centres, axis=0), preferred_element_type=f32)
            product = product.astype(bf16)
            at = g * 64 + n * 8
            prefix_ref[at : at + 16, :128] = product[:16]
            prefix_ref[at : at + 16, 128:] = product[16:]

    def contract(i, g):
        tails = [
            jnp.concatenate(
                [last_ref[index(i, 4 + j, n * groups + e)] for e in (g, g + 1) for n in range(8)],
                axis=0,
            )
            for j in range(BAG)
        ]
        product = lax.dot_general(
            prefix_ref[g * 64 : g * 64 + 128, :],
            jnp.concatenate(tails, axis=1),
            (((1,), (1,)), ((), ())),
            preferred_element_type=f32,
        )
        for e in range(2):
            own = product[e * 64 : e * 64 + 64, e * 128 : e * 128 + 128]
            mixed = own[:8]
            for n in range(1, 8):
                mixed = jnp.where(lane == n, own[n * 8 : n * 8 + 8], mixed)
            mixed_ref[(g + e) * 8 : (g + e) * 8 + 8, :] = mixed

    def arrange(i, h):
        parts = [mixed_ref[pl.ds(h * 8 + a, 8, stride=8), :] for a in range(8)]
        for k in (1, 2, 4):
            low = (lane & k) == 0
            moved = list(parts)
            for a in range(8):
                if a & k == 0:
                    p, q = parts[a], parts[a + k]
                    moved[a] = jnp.where(low, p, pltpu.roll(q, 16 * k, 1))
                    moved[a + k] = jnp.where(low, pltpu.roll(p, 128 - 16 * k, 1), q)
            parts = moved
        for n in range(8):
            at = n * groups + h
            out_ref[i * per_block + at // part, at % part : at % part + 8, :] = parts[n].astype(bf16)

    def step(i, carry):
        now = jnp.minimum(i, blocks - 1)
        before = jnp.clip(i - 1, 0, blocks - 1)
        earlier = jnp.clip(i - 2, 0, blocks - 1)
        for h in range(0, groups, 8):
            arrange(earlier, h)
        for g in range(0, groups, 2):
            contract(before, g)
            prefixes(now, g)
            prefixes(now, g + 1)
        return carry

    lax.fori_loop(0, blocks + 2, step, 0)


def table_rows(got, head, middle, tail):
    senders, own = got.shape[0], got.shape[-1]
    lookups = senders * own * BAG
    vmem = pl.BlockSpec(memory_space=pltpu.VMEM)
    return pl.pallas_call(
        rows_kernel,
        out_shape=jax.ShapeDtypeStruct((senders, own, WIDTH), jnp.bfloat16),
        in_specs=[pl.BlockSpec(memory_space=pltpu.SMEM), vmem, vmem, vmem],
        out_specs=vmem,
        scratch_shapes=[
            pltpu.VMEM((BLOCK * 8, 256), jnp.bfloat16),
            pltpu.VMEM((BLOCK, 128), jnp.float32),
        ],
        compiler_params=pltpu.CompilerParams(vmem_limit_bytes=32 << 20),
        cost_estimate=pl.CostEstimate(
            flops=lookups * 2000000, bytes_accessed=6 << 20, transcendentals=0
        ),
    )(got, head, middle, tail)


def product_kernel(place_ref, rows_ref, grad_ref, own_ref, *refs):
    others, (held_ref, total_ref, sems) = refs[:-3], refs[-3:]
    chunks, size, _ = held_ref.shape
    copies = []
    for i in range(chunks):
        source = grad_ref.at[pl.ds(i * size, size)]
        copies.append(pltpu.make_async_copy(source, held_ref.at[i], sems.at[i]))
        copies[-1].start()
    for i in range(chunks):
        copies[i].wait()
        value = lax.dot_general(
            rows_ref[i * size : (i + 1) * size, :],
            held_ref[i],
            (((0,), (0,)), ((), ())),
            preferred_element_type=jnp.float32,
        )
        if i == 0:
            total_ref[...] = value
        else:
            total_ref[...] += value
    columns = own_ref.shape[1]
    parts = len(others) + 1
    for k in range(parts):
        at = pl.multiple_of(lax.rem(place_ref[0] + k, parts) * columns, columns)
        block = total_ref[:, pl.ds(at, columns)]
        if k == 0:
            own_ref[...] = block
        else:
            others[k - 1][...] = block.astype(jnp.bfloat16)


def partial_product(rows, grad, place, parts):
    samples, width = rows.shape
    hidden_units = grad.shape[1]
    size = min(samples, 512)
    vmem = pl.BlockSpec(memory_space=pltpu.VMEM)
    return pl.pallas_call(
        product_kernel,
        out_shape=[jax.ShapeDtypeStruct((width, hidden_units // parts), jnp.float32)]
        + [jax.ShapeDtypeStruct((width, hidden_units // parts), jnp.bfloat16)] * (parts - 1),
        in_specs=[
            pl.BlockSpec(memory_space=pltpu.SMEM),
            vmem,
            pl.BlockSpec(memory_space=pltpu.HBM),
        ],
        out_specs=[vmem] * parts,
        scratch_shapes=[
            pltpu.VMEM((samples // size, size, hidden_units), grad.dtype),
            pltpu.VMEM((width, hidden_units), jnp.float32),
            pltpu.SemaphoreType.DMA((samples // size,)),
        ],
        compiler_params=pltpu.CompilerParams(vmem_limit_bytes=50 << 20),
        cost_estimate=pl.CostEstimate(
            flops=2 * samples * width * hidden_units,
            bytes_accessed=2 * samples * (width + hidden_units),
            transcendentals=0,
        ),
    )(place, rows, grad)


def body(core_ids, bag_lengths, first_core, middle_core, last_core, grad_hidden):
    own, tables = bag_lengths.shape
    ncore = first_core.shape[1]
    n_data = lax.axis_size("dp")

    gathered = lax.all_gather(grad_hidden, "table", axis=0, tiled=True)

    ids = jnp.transpose(core_ids, (1, 2, 3, 0))
    lengths = jnp.transpose(bag_lengths)[:, None, None, :]
    core = lax.broadcasted_iota(jnp.int32, ids.shape, 1)
    slot = lax.broadcasted_iota(jnp.int32, ids.shape, 2)
    sent = jnp.where((core == 0) & (slot >= lengths), ncore, ids)
    got = lax.all_to_all(sent, "table", split_axis=0, concat_axis=0, tiled=True)

    head = first_core[0].reshape(ncore, D1, RANK).astype(jnp.float32)
    head = jnp.pad(jnp.concatenate([head, head], axis=2), ((0, 8), (0, 0), (0, 0)))
    tail = last_core[0].reshape(ncore, RANK, D3).transpose(0, 2, 1)
    blank = jnp.zeros_like(tail)
    tail = jnp.concatenate(
        [jnp.concatenate([tail, blank], axis=2), jnp.concatenate([blank, tail], axis=2)], axis=1
    )
    rows = table_rows(got, head, middle_core[0], tail)

    returned = lax.all_to_all(rows, "table", split_axis=0, concat_axis=0, tiled=True)

    place = lax.axis_index("dp").astype(jnp.int32).reshape(1)
    weight_grad, *others = partial_product(rows.reshape(tables * own, WIDTH), gathered, place, n_data)
    for k, other in enumerate(others, 1):
        came = lax.ppermute(other, "dp", [(i, (i + k) % n_data) for i in range(n_data)])
        weight_grad = weight_grad + came.astype(jnp.float32)

    pooled = jnp.transpose(returned, (1, 0, 2)).reshape(own, tables * WIDTH)
    return (pooled, weight_grad)


def solution(mesh):
    placed = (
        P(("dp", "table"), None, None, None),
        P(("dp", "table"), None),
        P("table", None, None),
        P("table", None, None, None),
        P("table", None, None),
        P(("dp", "table"), None),
    )
    return jax.shard_map(
        body,
        mesh=mesh,
        in_specs=placed,
        out_specs=(P(("dp", "table"), None), P("table", "dp")),
        check_vma=False,
    )
```

```python
import functools

import jax
import jax.numpy as jnp
from jax import lax
from jax.experimental import pallas as pl
from jax.experimental.pallas import tpu as pltpu
from jax.sharding import PartitionSpec as P

D1 = 8
D2 = 2
D3 = 8
RANK = 64
BAG = 2
WIDTH = D1 * D2 * D3
BLOCK = 128


def rows_kernel(ids_ref, first_ref, middle_ref, last_ref, out_ref, prefix_ref, mixed_ref):
    f32 = jnp.float32
    bf16 = jnp.bfloat16
    senders, part, _ = out_ref.shape
    per_block = BLOCK // part
    blocks = senders // per_block
    groups = BLOCK // 8
    row16 = lax.broadcasted_iota(jnp.int32, (16, 128), 0)
    lane16 = lax.broadcasted_iota(jnp.int32, (16, 128), 1)
    keep = ((row16 < 8) == (lane16 < 64)).astype(bf16)
    lane = lax.broadcasted_iota(jnp.int32, (8, 128), 1) // 16

    def index(i, word, sample):
        return ids_ref[i * per_block + sample // part, word // BAG, word % BAG, sample % part]

    def prefixes(i, g):
        for n in range(0, 8, 4):
            at = g * 64 + n * 8
            for j in range(BAG):
                left, right = [], []
                for m in (n, n + 2):
                    pair = (m * groups + g, (m + 1) * groups + g)
                    two = [first_ref[index(i, j, a)] for a in pair]
                    left.append(jnp.concatenate(two, axis=0).astype(bf16) * keep)
                    two = [middle_ref[index(i, 2 + j, a)] for a in pair]
                    right.append(jnp.concatenate(two, axis=0))
                product = jnp.dot(
                    jnp.concatenate(left, axis=0),
                    jnp.concatenate(right, axis=1),
                    preferred_element_type=f32,
                ).astype(bf16)
                prefix_ref[at : at + 16, j * 128 : j * 128 + 128] = product[:16, :128]
                prefix_ref[at + 16 : at + 32, j * 128 : j * 128 + 128] = product[16:, 128:]

    def contract(i, g):
        tails = [
            jnp.concatenate(
                [last_ref[index(i, 4 + j, n * groups + e)] for e in (g, g + 1) for n in range(8)],
                axis=0,
            )
            for j in range(BAG)
        ]
        product = lax.dot_general(
            prefix_ref[g * 64 : g * 64 + 128, :],
            jnp.concatenate(tails, axis=1),
            (((1,), (1,)), ((), ())),
            preferred_element_type=f32,
        )
        for e in range(2):
            own = product[e * 64 : e * 64 + 64, e * 128 : e * 128 + 128]
            mixed = own[:8]
            for n in range(1, 8):
                mixed = jnp.where(lane == n, own[n * 8 : n * 8 + 8], mixed)
            mixed_ref[(g + e) * 8 : (g + e) * 8 + 8, :] = mixed

    def arrange(i, h):
        parts = [mixed_ref[pl.ds(h * 8 + a, 8, stride=8), :] for a in range(8)]
        for k in (1, 2, 4):
            low = (lane & k) == 0
            moved = list(parts)
            for a in range(8):
                if a & k == 0:
                    p, q = parts[a], parts[a + k]
                    moved[a] = jnp.where(low, p, pltpu.roll(q, 16 * k, 1))
                    moved[a + k] = jnp.where(low, pltpu.roll(p, 128 - 16 * k, 1), q)
            parts = moved
        for n in range(8):
            at = n * groups + h
            out_ref[i * per_block + at // part, at % part : at % part + 8, :] = parts[n].astype(bf16)

    def step(now, before, earlier):
        if earlier is not None:
            for h in range(0, groups, 8):
                arrange(earlier, h)
        for g in range(0, groups, 2):
            if before is not None:
                contract(before, g)
            if now is not None:
                prefixes(now, g)
                prefixes(now, g + 1)

    def steady(i, carry):
        step(i, i - 1, i - 2)
        return carry

    step(0, None, None)
    step(1, 0, None)
    lax.fori_loop(2, blocks, steady, 0, unroll=2)
    step(None, blocks - 1, blocks - 2)
    step(None, None, blocks - 1)


def table_rows(got, head, middle, tail):
    senders, own = got.shape[0], got.shape[-1]
    lookups = senders * own * BAG
    vmem = pl.BlockSpec(memory_space=pltpu.VMEM)
    return pl.pallas_call(
        rows_kernel,
        out_shape=jax.ShapeDtypeStruct((senders, own, WIDTH), jnp.bfloat16),
        in_specs=[pl.BlockSpec(memory_space=pltpu.SMEM), vmem, vmem, vmem],
        out_specs=vmem,
        scratch_shapes=[
            pltpu.VMEM((BLOCK * 8, 256), jnp.bfloat16),
            pltpu.VMEM((BLOCK, 128), jnp.float32),
        ],
        compiler_params=pltpu.CompilerParams(vmem_limit_bytes=32 << 20),
        cost_estimate=pl.CostEstimate(
            flops=lookups * 2000000, bytes_accessed=6 << 20, transcendentals=0
        ),
    )(got, head, middle, tail)


def product_kernel(place_ref, rows_ref, grad_ref, own_ref, *refs):
    others, (held_ref, total_ref, sems) = refs[:-3], refs[-3:]
    chunks, size, _ = held_ref.shape
    copies = []
    for i in range(chunks):
        source = grad_ref.at[pl.ds(i * size, size)]
        copies.append(pltpu.make_async_copy(source, held_ref.at[i], sems.at[i]))
        copies[-1].start()
    for i in range(chunks):
        copies[i].wait()
        value = lax.dot_general(
            rows_ref[i * size : (i + 1) * size, :],
            held_ref[i],
            (((0,), (0,)), ((), ())),
            preferred_element_type=jnp.float32,
        )
        if i == 0:
            total_ref[...] = value
        else:
            total_ref[...] += value
    columns = own_ref.shape[1]
    parts = len(others) + 1
    for k in range(parts):
        at = pl.multiple_of(lax.rem(place_ref[0] + k, parts) * columns, columns)
        block = total_ref[:, pl.ds(at, columns)]
        if k == 0:
            own_ref[...] = block
        else:
            others[k - 1][...] = block.astype(jnp.bfloat16)


def partial_product(rows, grad, place, parts):
    samples, width = rows.shape
    hidden_units = grad.shape[1]
    size = min(samples, 512)
    vmem = pl.BlockSpec(memory_space=pltpu.VMEM)
    return pl.pallas_call(
        product_kernel,
        out_shape=[jax.ShapeDtypeStruct((width, hidden_units // parts), jnp.float32)]
        + [jax.ShapeDtypeStruct((width, hidden_units // parts), jnp.bfloat16)] * (parts - 1),
        in_specs=[
            pl.BlockSpec(memory_space=pltpu.SMEM),
            vmem,
            pl.BlockSpec(memory_space=pltpu.HBM),
        ],
        out_specs=[vmem] * parts,
        scratch_shapes=[
            pltpu.VMEM((samples // size, size, hidden_units), grad.dtype),
            pltpu.VMEM((width, hidden_units), jnp.float32),
            pltpu.SemaphoreType.DMA((samples // size,)),
        ],
        compiler_params=pltpu.CompilerParams(vmem_limit_bytes=50 << 20),
        cost_estimate=pl.CostEstimate(
            flops=2 * samples * width * hidden_units,
            bytes_accessed=2 * samples * (width + hidden_units),
            transcendentals=0,
        ),
    )(place, rows, grad)


def mask_kernel(ids_ref, lengths_ref, out_ref, *, unused):
    slot = lax.broadcasted_iota(jnp.int32, ids_ref.shape[:1] + ids_ref.shape[2:], 1)
    out_ref[:, 1:] = ids_ref[:, 1:]
    out_ref[:, 0] = jnp.where(slot < lengths_ref[...][:, None, :], ids_ref[:, 0], unused)


def masked(ids, lengths, unused):
    vmem = pl.BlockSpec(memory_space=pltpu.VMEM)
    return pl.pallas_call(
        functools.partial(mask_kernel, unused=unused),
        out_shape=jax.ShapeDtypeStruct(ids.shape, ids.dtype),
        in_specs=[vmem, vmem],
        out_specs=vmem,
    )(ids, lengths)


def beside_kernel(blocks_ref, out_ref, sems):
    tables, _, width = blocks_ref.shape
    copies = []
    for t in range(tables):
        target = out_ref.at[:, pl.ds(t * width, width)]
        copies.append(pltpu.make_async_copy(blocks_ref.at[t], target, sems.at[t]))
        copies[-1].start()
    for copy in copies:
        copy.wait()


def side_by_side(blocks):
    tables, own, width = blocks.shape
    return pl.pallas_call(
        beside_kernel,
        out_shape=jax.ShapeDtypeStruct((own, tables * width), blocks.dtype),
        in_specs=[pl.BlockSpec(memory_space=pl.ANY)],
        out_specs=pl.BlockSpec(memory_space=pl.ANY),
        scratch_shapes=[pltpu.SemaphoreType.DMA((tables,))],
    )(blocks)


def body(core_ids, bag_lengths, first_core, middle_core, last_core, grad_hidden):
    own, tables = bag_lengths.shape
    ncore = first_core.shape[1]
    n_data = lax.axis_size("dp")

    gathered = lax.all_gather(grad_hidden, "table", axis=0, tiled=True)

    sent = masked(jnp.transpose(core_ids, (1, 2, 3, 0)), jnp.transpose(bag_lengths), ncore)
    got = lax.all_to_all(sent, "table", split_axis=0, concat_axis=0, tiled=True)

    head = first_core[0].reshape(ncore, D1, RANK).astype(jnp.float32)
    head = jnp.pad(jnp.concatenate([head, head], axis=2), ((0, 8), (0, 0), (0, 0)))
    tail = last_core[0].reshape(ncore, RANK, D3).transpose(0, 2, 1)
    blank = jnp.zeros_like(tail)
    tail = jnp.concatenate(
        [jnp.concatenate([tail, blank], axis=2), jnp.concatenate([blank, tail], axis=2)], axis=1
    )
    rows = table_rows(got, head, middle_core[0], tail)

    returned = lax.all_to_all(rows, "table", split_axis=0, concat_axis=0, tiled=True)

    place = lax.axis_index("dp").astype(jnp.int32).reshape(1)
    weight_grad, *others = partial_product(rows.reshape(tables * own, WIDTH), gathered, place, n_data)
    for k, other in enumerate(others, 1):
        came = lax.ppermute(other, "dp", [(i, (i + k) % n_data) for i in range(n_data)])
        weight_grad = weight_grad + came.astype(jnp.float32)

    returned, weight_grad = lax.optimization_barrier((returned, weight_grad))
    pooled = side_by_side(returned)
    return (pooled, weight_grad)


def solution(mesh):
    placed = (
        P(("dp", "table"), None, None, None),
        P(("dp", "table"), None),
        P("table", None, None),
        P("table", None, None, None),
        P("table", None, None),
        P(("dp", "table"), None),
    )
    return jax.shard_map(
        body,
        mesh=mesh,
        in_specs=placed,
        out_specs=(P(("dp", "table"), None), P("table", "dp")),
        check_vma=False,
    )
```

```python
import functools

import jax
import jax.numpy as jnp
from jax import lax
from jax.experimental import pallas as pl
from jax.experimental.pallas import tpu as pltpu
from jax.sharding import PartitionSpec as P

D1 = 8
D2 = 2
D3 = 8
RANK = 64
BAG = 2
WIDTH = D1 * D2 * D3
BLOCK = 128


def rows_kernel(ids_ref, first_ref, middle_ref, last_ref, out_ref, prefix_ref, mixed_ref):
    f32 = jnp.float32
    bf16 = jnp.bfloat16
    senders, part, _ = out_ref.shape
    per_block = BLOCK // part
    blocks = senders // per_block
    groups = BLOCK // 8
    row16 = lax.broadcasted_iota(jnp.int32, (16, 128), 0)
    lane16 = lax.broadcasted_iota(jnp.int32, (16, 128), 1)
    keep = ((row16 < 8) == (lane16 < 64)).astype(bf16)
    lane = lax.broadcasted_iota(jnp.int32, (8, 128), 1) // 16

    def index(i, word, sample):
        return ids_ref[i * per_block + sample // part, word // BAG, word % BAG, sample % part]

    def prefixes(i, g):
        for n in range(0, 8, 4):
            at = g * 64 + n * 8
            for j in range(BAG):
                left, right = [], []
                for m in (n, n + 2):
                    pair = (m * groups + g, (m + 1) * groups + g)
                    two = [first_ref[index(i, j, a)] for a in pair]
                    left.append(jnp.concatenate(two, axis=0).astype(bf16) * keep)
                    two = [middle_ref[index(i, 2 + j, a)] for a in pair]
                    right.append(jnp.concatenate(two, axis=0))
                product = jnp.dot(
                    jnp.concatenate(left, axis=0),
                    jnp.concatenate(right, axis=1),
                    preferred_element_type=f32,
                ).astype(bf16)
                prefix_ref[at : at + 16, j * 128 : j * 128 + 128] = product[:16, :128]
                prefix_ref[at + 16 : at + 32, j * 128 : j * 128 + 128] = product[16:, 128:]

    def contract(i, g):
        tails = [
            jnp.concatenate(
                [last_ref[index(i, 4 + j, n * groups + e)] for e in (g, g + 1) for n in range(8)],
                axis=0,
            )
            for j in range(BAG)
        ]
        product = lax.dot_general(
            prefix_ref[g * 64 : g * 64 + 128, :],
            jnp.concatenate(tails, axis=1),
            (((1,), (1,)), ((), ())),
            preferred_element_type=f32,
        )
        for e in range(2):
            own = product[e * 64 : e * 64 + 64, e * 128 : e * 128 + 128]
            mixed = own[:8]
            for n in range(1, 8):
                mixed = jnp.where(lane == n, own[n * 8 : n * 8 + 8], mixed)
            mixed_ref[(g + e) * 8 : (g + e) * 8 + 8, :] = mixed

    def arrange(i, h):
        parts = [mixed_ref[pl.ds(h * 8 + a, 8, stride=8), :] for a in range(8)]
        for k in (1, 2, 4):
            low = (lane & k) == 0
            moved = list(parts)
            for a in range(8):
                if a & k == 0:
                    p, q = parts[a], parts[a + k]
                    moved[a] = jnp.where(low, p, pltpu.roll(q, 16 * k, 1))
                    moved[a + k] = jnp.where(low, pltpu.roll(p, 128 - 16 * k, 1), q)
            parts = moved
        for n in range(8):
            at = n * groups + h
            out_ref[i * per_block + at // part, at % part : at % part + 8, :] = parts[n].astype(bf16)

    def step(now, before, earlier):
        if earlier is not None:
            for h in range(0, groups, 8):
                arrange(earlier, h)
        for g in range(0, groups, 2):
            if before is not None:
                contract(before, g)
            if now is not None:
                prefixes(now, g)
                prefixes(now, g + 1)

    def steady(i, carry):
        step(i, i - 1, i - 2)
        return carry

    step(0, None, None)
    step(1, 0, None)
    lax.fori_loop(2, blocks, steady, 0, unroll=2)
    step(None, blocks - 1, blocks - 2)
    step(None, None, blocks - 1)


def table_rows(got, head, middle, tail):
    senders, own = got.shape[0], got.shape[-1]
    lookups = senders * own * BAG
    vmem = pl.BlockSpec(memory_space=pltpu.VMEM)
    return pl.pallas_call(
        rows_kernel,
        out_shape=jax.ShapeDtypeStruct((senders, own, WIDTH), jnp.bfloat16),
        in_specs=[pl.BlockSpec(memory_space=pltpu.SMEM), vmem, vmem, vmem],
        out_specs=vmem,
        scratch_shapes=[
            pltpu.VMEM((BLOCK * 8, 256), jnp.bfloat16),
            pltpu.VMEM((BLOCK, 128), jnp.float32),
        ],
        compiler_params=pltpu.CompilerParams(vmem_limit_bytes=32 << 20),
        cost_estimate=pl.CostEstimate(
            flops=lookups * 2000000, bytes_accessed=6 << 20, transcendentals=0
        ),
    )(got, head, middle, tail)


def product_kernel(place_ref, rows_ref, grad_ref, own_ref, *refs):
    others, (held_ref, total_ref, sems) = refs[:-3], refs[-3:]
    chunks, size, _ = held_ref.shape
    copies = []
    for i in range(chunks):
        source = grad_ref.at[pl.ds(i * size, size)]
        copies.append(pltpu.make_async_copy(source, held_ref.at[i], sems.at[i]))
        copies[-1].start()
    for i in range(chunks):
        copies[i].wait()
        value = lax.dot_general(
            rows_ref[i * size : (i + 1) * size, :],
            held_ref[i],
            (((0,), (0,)), ((), ())),
            preferred_element_type=jnp.float32,
        )
        if i == 0:
            total_ref[...] = value
        else:
            total_ref[...] += value
    columns = own_ref.shape[1]
    parts = len(others) + 1
    for k in range(parts):
        at = pl.multiple_of(lax.rem(place_ref[0] + k, parts) * columns, columns)
        block = total_ref[:, pl.ds(at, columns)]
        if k == 0:
            own_ref[...] = block
        else:
            others[k - 1][...] = block.astype(jnp.bfloat16)


def partial_product(rows, grad, place, parts):
    samples, width = rows.shape
    hidden_units = grad.shape[1]
    size = min(samples, 512)
    vmem = pl.BlockSpec(memory_space=pltpu.VMEM)
    return pl.pallas_call(
        product_kernel,
        out_shape=[jax.ShapeDtypeStruct((width, hidden_units // parts), jnp.float32)]
        + [jax.ShapeDtypeStruct((width, hidden_units // parts), jnp.bfloat16)] * (parts - 1),
        in_specs=[
            pl.BlockSpec(memory_space=pltpu.SMEM),
            vmem,
            pl.BlockSpec(memory_space=pltpu.HBM),
        ],
        out_specs=[vmem] * parts,
        scratch_shapes=[
            pltpu.VMEM((samples // size, size, hidden_units), grad.dtype),
            pltpu.VMEM((width, hidden_units), jnp.float32),
            pltpu.SemaphoreType.DMA((samples // size,)),
        ],
        compiler_params=pltpu.CompilerParams(vmem_limit_bytes=50 << 20),
        cost_estimate=pl.CostEstimate(
            flops=2 * samples * width * hidden_units,
            bytes_accessed=2 * samples * (width + hidden_units),
            transcendentals=0,
        ),
    )(place, rows, grad)


def mask_kernel(ids_ref, lengths_ref, out_ref, *, unused):
    slot = lax.broadcasted_iota(jnp.int32, ids_ref.shape[:1] + ids_ref.shape[2:], 1)
    out_ref[:, 1:] = ids_ref[:, 1:]
    out_ref[:, 0] = jnp.where(slot < lengths_ref[...][:, None, :], ids_ref[:, 0], unused)


def masked(ids, lengths, unused):
    vmem = pl.BlockSpec(memory_space=pltpu.VMEM)
    return pl.pallas_call(
        functools.partial(mask_kernel, unused=unused),
        out_shape=jax.ShapeDtypeStruct(ids.shape, ids.dtype),
        in_specs=[vmem, vmem],
        out_specs=vmem,
        compiler_params=pltpu.CompilerParams(vmem_limit_bytes=2 << 20),
    )(ids, lengths)


def beside_kernel(blocks_ref, out_ref, rows_ref, sems):
    tables, _, width = blocks_ref.shape
    pieces, size, _ = rows_ref.shape
    copies = []
    for p in range(pieces):
        for t in range(tables):
            rows_ref[p, :, t * width : (t + 1) * width] = blocks_ref[t, p * size : (p + 1) * size]
        target = out_ref.at[pl.ds(p * size, size)]
        copies.append(pltpu.make_async_copy(rows_ref.at[p], target, sems.at[p]))
        copies[-1].start()
    for copy in copies:
        copy.wait()


def side_by_side(blocks):
    tables, own, width = blocks.shape
    pieces = own // 16
    return pl.pallas_call(
        beside_kernel,
        out_shape=jax.ShapeDtypeStruct((own, tables * width), blocks.dtype),
        in_specs=[pl.BlockSpec(memory_space=pltpu.VMEM)],
        out_specs=pl.BlockSpec(memory_space=pl.ANY),
        scratch_shapes=[
            pltpu.VMEM((pieces, own // pieces, tables * width), blocks.dtype),
            pltpu.SemaphoreType.DMA((pieces,)),
        ],
        compiler_params=pltpu.CompilerParams(vmem_limit_bytes=4 << 20),
    )(blocks)


def body(core_ids, bag_lengths, first_core, middle_core, last_core, grad_hidden):
    own, tables = bag_lengths.shape
    ncore = first_core.shape[1]
    n_data = lax.axis_size("dp")

    gathered = lax.all_gather(grad_hidden, "table", axis=0, tiled=True)

    sent = masked(jnp.transpose(core_ids, (1, 2, 3, 0)), jnp.transpose(bag_lengths), ncore)
    got = lax.all_to_all(sent, "table", split_axis=0, concat_axis=0, tiled=True)

    head = first_core[0].reshape(ncore, D1, RANK).astype(jnp.float32)
    head = jnp.pad(jnp.concatenate([head, head], axis=2), ((0, 8), (0, 0), (0, 0)))
    tail = last_core[0].reshape(ncore, RANK, D3).transpose(0, 2, 1)
    blank = jnp.zeros_like(tail)
    tail = jnp.concatenate(
        [jnp.concatenate([tail, blank], axis=2), jnp.concatenate([blank, tail], axis=2)], axis=1
    )
    rows = table_rows(got, head, middle_core[0], tail)

    returned = lax.all_to_all(rows, "table", split_axis=0, concat_axis=0, tiled=True)

    place = lax.axis_index("dp").astype(jnp.int32).reshape(1)
    weight_grad, *others = partial_product(rows.reshape(tables * own, WIDTH), gathered, place, n_data)
    for k, other in enumerate(others, 1):
        came = lax.ppermute(other, "dp", [(i, (i + k) % n_data) for i in range(n_data)])
        weight_grad = weight_grad + came.astype(jnp.float32)

    returned, weight_grad = lax.optimization_barrier((returned, weight_grad))
    pooled = side_by_side(returned)
    return (pooled, weight_grad)


def solution(mesh):
    placed = (
        P(("dp", "table"), None, None, None),
        P(("dp", "table"), None),
        P("table", None, None),
        P("table", None, None, None),
        P("table", None, None),
        P(("dp", "table"), None),
    )
    return jax.shard_map(
        body,
        mesh=mesh,
        in_specs=placed,
        out_specs=(P(("dp", "table"), None), P("table", "dp")),
        check_vma=False,
    )
```

```python
import functools

import jax
import jax.numpy as jnp
from jax import lax
from jax.experimental import pallas as pl
from jax.experimental.pallas import tpu as pltpu
from jax.sharding import PartitionSpec as P

D1 = 8
D2 = 2
D3 = 8
RANK = 64
BAG = 2
WIDTH = D1 * D2 * D3
BLOCK = 128
FETCHES = 5


def rows_kernel(
    got_ref, first_ref, core_ref, last_ref, out_ref, prefix_ref, mixed_ref, middle_ref, ids_ref, sems
):
    f32 = jnp.float32
    bf16 = jnp.bfloat16
    senders, part, _ = out_ref.shape
    per_block = BLOCK // part
    blocks = senders // per_block
    groups = BLOCK // 8
    row16 = lax.broadcasted_iota(jnp.int32, (16, 128), 0)
    lane16 = lax.broadcasted_iota(jnp.int32, (16, 128), 1)
    keep = ((row16 < 8) == (lane16 < 64)).astype(bf16)
    lane = lax.broadcasted_iota(jnp.int32, (8, 128), 1) // 16

    size = core_ref.shape[0] // FETCHES
    copies = [pltpu.make_async_copy(got_ref, ids_ref, sems.at[FETCHES])]
    for f in range(FETCHES):
        part_of = pl.ds(f * size, size)
        copies.append(
            pltpu.make_async_copy(core_ref.at[part_of], middle_ref.at[part_of], sems.at[f])
        )
    for copy in copies:
        copy.start()
    for copy in copies:
        copy.wait()

    def index(i, word, sample):
        return ids_ref[i * per_block + sample // part, word // BAG, word % BAG, sample % part]

    def prefixes(i, g):
        for n in range(0, 8, 4):
            at = g * 64 + n * 8
            for j in range(BAG):
                left, right = [], []
                for m in (n, n + 2):
                    pair = (m * groups + g, (m + 1) * groups + g)
                    two = [first_ref[index(i, j, a)] for a in pair]
                    left.append(jnp.concatenate(two, axis=0).astype(bf16) * keep)
                    two = [middle_ref[index(i, 2 + j, a)] for a in pair]
                    right.append(jnp.concatenate(two, axis=0))
                product = jnp.dot(
                    jnp.concatenate(left, axis=0),
                    jnp.concatenate(right, axis=1),
                    preferred_element_type=f32,
                ).astype(bf16)
                prefix_ref[at : at + 16, j * 128 : j * 128 + 128] = product[:16, :128]
                prefix_ref[at + 16 : at + 32, j * 128 : j * 128 + 128] = product[16:, 128:]

    def contract(i, g):
        tails = [
            jnp.concatenate(
                [last_ref[index(i, 4 + j, n * groups + e)] for e in (g, g + 1) for n in range(8)],
                axis=0,
            )
            for j in range(BAG)
        ]
        product = lax.dot_general(
            prefix_ref[g * 64 : g * 64 + 128, :],
            jnp.concatenate(tails, axis=1),
            (((1,), (1,)), ((), ())),
            preferred_element_type=f32,
        )
        for e in range(2):
            own = product[e * 64 : e * 64 + 64, e * 128 : e * 128 + 128]
            mixed = own[:8]
            for n in range(1, 8):
                mixed = jnp.where(lane == n, own[n * 8 : n * 8 + 8], mixed)
            mixed_ref[(g + e) * 8 : (g + e) * 8 + 8, :] = mixed

    def arrange(i, h):
        parts = [mixed_ref[pl.ds(h * 8 + a, 8, stride=8), :] for a in range(8)]
        for k in (1, 2, 4):
            low = (lane & k) == 0
            moved = list(parts)
            for a in range(8):
                if a & k == 0:
                    p, q = parts[a], parts[a + k]
                    moved[a] = jnp.where(low, p, pltpu.roll(q, 16 * k, 1))
                    moved[a + k] = jnp.where(low, pltpu.roll(p, 128 - 16 * k, 1), q)
            parts = moved
        for n in range(8):
            at = n * groups + h
            out_ref[i * per_block + at // part, at % part : at % part + 8, :] = parts[n].astype(bf16)

    def step(now, before, earlier):
        if earlier is not None:
            for h in range(0, groups, 8):
                arrange(earlier, h)
        for g in range(0, groups, 2):
            if before is not None:
                contract(before, g)
            if now is not None:
                prefixes(now, g)
                prefixes(now, g + 1)

    def steady(i, carry):
        step(i, i - 1, i - 2)
        return carry

    step(0, None, None)
    step(1, 0, None)
    lax.fori_loop(2, blocks, steady, 0, unroll=2)
    step(None, blocks - 1, blocks - 2)
    step(None, None, blocks - 1)


def table_rows(got, head, middle, tail):
    senders, own = got.shape[0], got.shape[-1]
    lookups = senders * own * BAG
    vmem = pl.BlockSpec(memory_space=pltpu.VMEM)
    return pl.pallas_call(
        rows_kernel,
        out_shape=jax.ShapeDtypeStruct((senders, own, WIDTH), jnp.bfloat16),
        in_specs=[pl.BlockSpec(memory_space=pl.ANY), vmem, pl.BlockSpec(memory_space=pl.ANY), vmem],
        out_specs=vmem,
        scratch_shapes=[
            pltpu.VMEM((BLOCK * 8, 256), jnp.bfloat16),
            pltpu.VMEM((BLOCK, 128), jnp.float32),
            pltpu.VMEM(middle.shape, middle.dtype),
            pltpu.SMEM(got.shape, got.dtype),
            pltpu.SemaphoreType.DMA((FETCHES + 1,)),
        ],
        compiler_params=pltpu.CompilerParams(vmem_limit_bytes=50 << 20),
        cost_estimate=pl.CostEstimate(
            flops=lookups * 2000000, bytes_accessed=6 << 20, transcendentals=0
        ),
    )(got, head, middle, tail)


def product_kernel(place_ref, rows_ref, grad_ref, own_ref, *refs):
    others, (held_ref, total_ref, sems) = refs[:-3], refs[-3:]
    chunks, size, _ = held_ref.shape
    copies = []
    for i in range(chunks):
        source = grad_ref.at[pl.ds(i * size, size)]
        copies.append(pltpu.make_async_copy(source, held_ref.at[i], sems.at[i]))
        copies[-1].start()
    for i in range(chunks):
        copies[i].wait()
        value = lax.dot_general(
            rows_ref[i * size : (i + 1) * size, :],
            held_ref[i],
            (((0,), (0,)), ((), ())),
            preferred_element_type=jnp.float32,
        )
        if i == 0:
            total_ref[...] = value
        else:
            total_ref[...] += value
    columns = own_ref.shape[1]
    parts = len(others) + 1
    for k in range(parts):
        at = pl.multiple_of(lax.rem(place_ref[0] + k, parts) * columns, columns)
        block = total_ref[:, pl.ds(at, columns)]
        if k == 0:
            own_ref[...] = block
        else:
            others[k - 1][...] = block.astype(jnp.bfloat16)


def partial_product(rows, grad, place, parts):
    samples, width = rows.shape
    hidden_units = grad.shape[1]
    size = min(samples, 512)
    vmem = pl.BlockSpec(memory_space=pltpu.VMEM)
    return pl.pallas_call(
        product_kernel,
        out_shape=[jax.ShapeDtypeStruct((width, hidden_units // parts), jnp.float32)]
        + [jax.ShapeDtypeStruct((width, hidden_units // parts), jnp.bfloat16)] * (parts - 1),
        in_specs=[
            pl.BlockSpec(memory_space=pltpu.SMEM),
            vmem,
            pl.BlockSpec(memory_space=pltpu.HBM),
        ],
        out_specs=[vmem] * parts,
        scratch_shapes=[
            pltpu.VMEM((samples // size, size, hidden_units), grad.dtype),
            pltpu.VMEM((width, hidden_units), jnp.float32),
            pltpu.SemaphoreType.DMA((samples // size,)),
        ],
        compiler_params=pltpu.CompilerParams(vmem_limit_bytes=50 << 20),
        cost_estimate=pl.CostEstimate(
            flops=2 * samples * width * hidden_units,
            bytes_accessed=2 * samples * (width + hidden_units),
            transcendentals=0,
        ),
    )(place, rows, grad)


def mask_kernel(ids_ref, lengths_ref, out_ref, *, unused):
    slot = lax.broadcasted_iota(jnp.int32, ids_ref.shape[:1] + ids_ref.shape[2:], 1)
    out_ref[:, 1:] = ids_ref[:, 1:]
    out_ref[:, 0] = jnp.where(slot < lengths_ref[...][:, None, :], ids_ref[:, 0], unused)


def masked(ids, lengths, unused):
    vmem = pl.BlockSpec(memory_space=pltpu.VMEM)
    return pl.pallas_call(
        functools.partial(mask_kernel, unused=unused),
        out_shape=jax.ShapeDtypeStruct(ids.shape, ids.dtype),
        in_specs=[vmem, vmem],
        out_specs=vmem,
    )(ids, lengths)


def beside_kernel(blocks_ref, out_ref, rows_ref, sems):
    tables, _, width = blocks_ref.shape
    pieces, size, _ = rows_ref.shape
    copies = []
    for p in range(pieces):
        for t in range(tables):
            rows_ref[p, :, t * width : (t + 1) * width] = blocks_ref[t, p * size : (p + 1) * size]
        target = out_ref.at[pl.ds(p * size, size)]
        copies.append(pltpu.make_async_copy(rows_ref.at[p], target, sems.at[p]))
        copies[-1].start()
    for copy in copies:
        copy.wait()


def side_by_side(blocks):
    tables, own, width = blocks.shape
    pieces = own // 16
    return pl.pallas_call(
        beside_kernel,
        out_shape=jax.ShapeDtypeStruct((own, tables * width), blocks.dtype),
        in_specs=[pl.BlockSpec(memory_space=pltpu.VMEM)],
        out_specs=pl.BlockSpec(memory_space=pl.ANY),
        scratch_shapes=[
            pltpu.VMEM((pieces, own // pieces, tables * width), blocks.dtype),
            pltpu.SemaphoreType.DMA((pieces,)),
        ],
        compiler_params=pltpu.CompilerParams(vmem_limit_bytes=4 << 20),
    )(blocks)


def body(core_ids, bag_lengths, first_core, middle_core, last_core, grad_hidden):
    own, tables = bag_lengths.shape
    ncore = first_core.shape[1]
    n_data = lax.axis_size("dp")

    gathered = lax.all_gather(grad_hidden, "table", axis=0, tiled=True)

    sent = masked(jnp.transpose(core_ids, (1, 2, 3, 0)), jnp.transpose(bag_lengths), ncore)
    got = lax.all_to_all(sent, "table", split_axis=0, concat_axis=0, tiled=True)

    head = first_core[0].reshape(ncore, D1, RANK).astype(jnp.float32)
    head = jnp.pad(jnp.concatenate([head, head], axis=2), ((0, 8), (0, 0), (0, 0)))
    tail = last_core[0].reshape(ncore, RANK, D3).transpose(0, 2, 1)
    blank = jnp.zeros_like(tail)
    tail = jnp.concatenate(
        [jnp.concatenate([tail, blank], axis=2), jnp.concatenate([blank, tail], axis=2)], axis=1
    )
    rows = table_rows(got, head, middle_core[0], tail)

    returned = lax.all_to_all(rows, "table", split_axis=0, concat_axis=0, tiled=True)

    place = lax.axis_index("dp").astype(jnp.int32).reshape(1)
    weight_grad, *others = partial_product(rows.reshape(tables * own, WIDTH), gathered, place, n_data)
    for k, other in enumerate(others, 1):
        came = lax.ppermute(other, "dp", [(i, (i + k) % n_data) for i in range(n_data)])
        weight_grad = weight_grad + came.astype(jnp.float32)

    returned, weight_grad = lax.optimization_barrier((returned, weight_grad))
    pooled = side_by_side(returned)
    return (pooled, weight_grad)


def solution(mesh):
    placed = (
        P(("dp", "table"), None, None, None),
        P(("dp", "table"), None),
        P("table", None, None),
        P("table", None, None, None),
        P("table", None, None),
        P(("dp", "table"), None),
    )
    return jax.shard_map(
        body,
        mesh=mesh,
        in_specs=placed,
        out_specs=(P(("dp", "table"), None), P("table", "dp")),
        check_vma=False,
    )
```

```python
import functools

import jax
import jax.numpy as jnp
from jax import lax
from jax.experimental import pallas as pl
from jax.experimental.pallas import tpu as pltpu
from jax.sharding import PartitionSpec as P

D1 = 8
D2 = 2
D3 = 8
RANK = 64
BAG = 2
WIDTH = D1 * D2 * D3
BLOCK = 128
FETCHES = 5


def rows_kernel(
    got_ref, first_ref, core_ref, last_ref, out_ref, prefix_ref, mixed_ref, middle_ref, ids_ref, sems
):
    f32 = jnp.float32
    bf16 = jnp.bfloat16
    senders, part, _ = out_ref.shape
    per_block = BLOCK // part
    blocks = senders // per_block
    groups = BLOCK // 8
    row16 = lax.broadcasted_iota(jnp.int32, (16, 128), 0)
    lane16 = lax.broadcasted_iota(jnp.int32, (16, 128), 1)
    keep = ((row16 < 8) == (lane16 < 64)).astype(bf16)
    lane = lax.broadcasted_iota(jnp.int32, (8, 128), 1) // 16

    size = core_ref.shape[0] // FETCHES
    copies = [pltpu.make_async_copy(got_ref, ids_ref, sems.at[FETCHES])]
    for f in range(FETCHES):
        part_of = pl.ds(f * size, size)
        copies.append(
            pltpu.make_async_copy(core_ref.at[part_of], middle_ref.at[part_of], sems.at[f])
        )
    for copy in copies:
        copy.start()
    for copy in copies:
        copy.wait()

    def index(i, word, sample):
        return ids_ref[i * per_block + sample // part, word // BAG, word % BAG, sample % part]

    def prefixes(i, g):
        for n in range(0, 8, 4):
            at = g * 64 + n * 8
            for j in range(BAG):
                left, right = [], []
                for m in (n, n + 2):
                    pair = (m * groups + g, (m + 1) * groups + g)
                    two = [first_ref[index(i, j, a)] for a in pair]
                    left.append(jnp.concatenate(two, axis=0).astype(bf16) * keep)
                    two = [middle_ref[index(i, 2 + j, a)] for a in pair]
                    right.append(jnp.concatenate(two, axis=0))
                product = jnp.dot(
                    jnp.concatenate(left, axis=0),
                    jnp.concatenate(right, axis=1),
                    preferred_element_type=f32,
                ).astype(bf16)
                prefix_ref[at : at + 16, j * 128 : j * 128 + 128] = product[:16, :128]
                prefix_ref[at + 16 : at + 32, j * 128 : j * 128 + 128] = product[16:, 128:]

    def contract(i, g):
        tails = [
            jnp.concatenate(
                [last_ref[index(i, 4 + j, n * groups + e)] for e in (g, g + 1) for n in range(8)],
                axis=0,
            )
            for j in range(BAG)
        ]
        product = lax.dot_general(
            prefix_ref[g * 64 : g * 64 + 128, :],
            jnp.concatenate(tails, axis=1),
            (((1,), (1,)), ((), ())),
            preferred_element_type=f32,
        )
        for e in range(2):
            own = product[e * 64 : e * 64 + 64, e * 128 : e * 128 + 128]
            mixed = own[:8]
            for n in range(1, 8):
                mixed = jnp.where(lane == n, own[n * 8 : n * 8 + 8], mixed)
            mixed_ref[(g + e) * 8 : (g + e) * 8 + 8, :] = mixed

    def arrange(i, h):
        parts = [mixed_ref[pl.ds(h * 8 + a, 8, stride=8), :] for a in range(8)]
        for k in (1, 2, 4):
            low = (lane & k) == 0
            moved = list(parts)
            for a in range(8):
                if a & k == 0:
                    p, q = parts[a], parts[a + k]
                    moved[a] = jnp.where(low, p, pltpu.roll(q, 16 * k, 1))
                    moved[a + k] = jnp.where(low, pltpu.roll(p, 128 - 16 * k, 1), q)
            parts = moved
        for n in range(8):
            at = n * groups + h
            out_ref[i * per_block + at // part, at % part : at % part + 8, :] = parts[n].astype(bf16)

    def step(now, before, earlier):
        if earlier is not None:
            for h in range(0, groups, 8):
                arrange(earlier, h)
        for g in range(0, groups, 2):
            if before is not None:
                contract(before, g)
            if now is not None:
                prefixes(now, g)
                prefixes(now, g + 1)

    def steady(i, carry):
        step(i, i - 1, i - 2)
        return carry

    step(0, None, None)
    step(1, 0, None)
    lax.fori_loop(2, blocks, steady, 0, unroll=5)
    step(None, blocks - 1, blocks - 2)
    step(None, None, blocks - 1)


def table_rows(got, head, middle, tail):
    senders, own = got.shape[0], got.shape[-1]
    lookups = senders * own * BAG
    vmem = pl.BlockSpec(memory_space=pltpu.VMEM)
    return pl.pallas_call(
        rows_kernel,
        out_shape=jax.ShapeDtypeStruct((senders, own, WIDTH), jnp.bfloat16),
        in_specs=[pl.BlockSpec(memory_space=pl.ANY), vmem, pl.BlockSpec(memory_space=pl.ANY), vmem],
        out_specs=vmem,
        scratch_shapes=[
            pltpu.VMEM((BLOCK * 8, 256), jnp.bfloat16),
            pltpu.VMEM((BLOCK, 128), jnp.float32),
            pltpu.VMEM(middle.shape, middle.dtype),
            pltpu.SMEM(got.shape, got.dtype),
            pltpu.SemaphoreType.DMA((FETCHES + 1,)),
        ],
        compiler_params=pltpu.CompilerParams(vmem_limit_bytes=50 << 20),
        cost_estimate=pl.CostEstimate(
            flops=lookups * 2000000, bytes_accessed=6 << 20, transcendentals=0
        ),
    )(got, head, middle, tail)


def product_kernel(place_ref, rows_ref, grad_ref, own_ref, *refs):
    others, (held_ref, total_ref, sems) = refs[:-3], refs[-3:]
    chunks, size, _ = held_ref.shape
    copies = []
    for i in range(chunks):
        source = grad_ref.at[pl.ds(i * size, size)]
        copies.append(pltpu.make_async_copy(source, held_ref.at[i], sems.at[i]))
        copies[-1].start()
    for i in range(chunks):
        copies[i].wait()
        value = lax.dot_general(
            rows_ref[i * size : (i + 1) * size, :],
            held_ref[i],
            (((0,), (0,)), ((), ())),
            preferred_element_type=jnp.float32,
        )
        if i == 0:
            total_ref[...] = value
        else:
            total_ref[...] += value
    columns = own_ref.shape[1]
    parts = len(others) + 1
    for k in range(parts):
        at = pl.multiple_of(lax.rem(place_ref[0] + k, parts) * columns, columns)
        block = total_ref[:, pl.ds(at, columns)]
        if k == 0:
            own_ref[...] = block
        else:
            others[k - 1][...] = block.astype(jnp.bfloat16)


def partial_product(rows, grad, place, parts):
    samples, width = rows.shape
    hidden_units = grad.shape[1]
    size = min(samples, 512)
    vmem = pl.BlockSpec(memory_space=pltpu.VMEM)
    return pl.pallas_call(
        product_kernel,
        out_shape=[jax.ShapeDtypeStruct((width, hidden_units // parts), jnp.float32)]
        + [jax.ShapeDtypeStruct((width, hidden_units // parts), jnp.bfloat16)] * (parts - 1),
        in_specs=[
            pl.BlockSpec(memory_space=pltpu.SMEM),
            vmem,
            pl.BlockSpec(memory_space=pltpu.HBM),
        ],
        out_specs=[vmem] * parts,
        scratch_shapes=[
            pltpu.VMEM((samples // size, size, hidden_units), grad.dtype),
            pltpu.VMEM((width, hidden_units), jnp.float32),
            pltpu.SemaphoreType.DMA((samples // size,)),
        ],
        compiler_params=pltpu.CompilerParams(vmem_limit_bytes=50 << 20),
        cost_estimate=pl.CostEstimate(
            flops=2 * samples * width * hidden_units,
            bytes_accessed=2 * samples * (width + hidden_units),
            transcendentals=0,
        ),
    )(place, rows, grad)


def mask_kernel(ids_ref, lengths_ref, out_ref, *, unused):
    slot = lax.broadcasted_iota(jnp.int32, ids_ref.shape[:1] + ids_ref.shape[2:], 1)
    out_ref[:, 1:] = ids_ref[:, 1:]
    out_ref[:, 0] = jnp.where(slot < lengths_ref[...][:, None, :], ids_ref[:, 0], unused)


def masked(ids, lengths, unused):
    vmem = pl.BlockSpec(memory_space=pltpu.VMEM)
    return pl.pallas_call(
        functools.partial(mask_kernel, unused=unused),
        out_shape=jax.ShapeDtypeStruct(ids.shape, ids.dtype),
        in_specs=[vmem, vmem],
        out_specs=vmem,
    )(ids, lengths)


def beside_kernel(blocks_ref, out_ref, rows_ref, sems):
    tables, _, width = blocks_ref.shape
    pieces, size, _ = rows_ref.shape
    copies = []
    for p in range(pieces):
        for t in range(tables):
            rows_ref[p, :, t * width : (t + 1) * width] = blocks_ref[t, p * size : (p + 1) * size]
        target = out_ref.at[pl.ds(p * size, size)]
        copies.append(pltpu.make_async_copy(rows_ref.at[p], target, sems.at[p]))
        copies[-1].start()
    for copy in copies:
        copy.wait()


def side_by_side(blocks):
    tables, own, width = blocks.shape
    pieces = own // 16
    return pl.pallas_call(
        beside_kernel,
        out_shape=jax.ShapeDtypeStruct((own, tables * width), blocks.dtype),
        in_specs=[pl.BlockSpec(memory_space=pltpu.VMEM)],
        out_specs=pl.BlockSpec(memory_space=pl.ANY),
        scratch_shapes=[
            pltpu.VMEM((pieces, own // pieces, tables * width), blocks.dtype),
            pltpu.SemaphoreType.DMA((pieces,)),
        ],
        compiler_params=pltpu.CompilerParams(vmem_limit_bytes=4 << 20),
    )(blocks)


def body(core_ids, bag_lengths, first_core, middle_core, last_core, grad_hidden):
    own, tables = bag_lengths.shape
    ncore = first_core.shape[1]
    n_data = lax.axis_size("dp")

    gathered = lax.all_gather(grad_hidden, "table", axis=0, tiled=True)

    sent = masked(jnp.transpose(core_ids, (1, 2, 3, 0)), jnp.transpose(bag_lengths), ncore)
    got = lax.all_to_all(sent, "table", split_axis=0, concat_axis=0, tiled=True)

    head = first_core[0].reshape(ncore, D1, RANK).astype(jnp.float32)
    head = jnp.pad(jnp.concatenate([head, head], axis=2), ((0, 8), (0, 0), (0, 0)))
    tail = last_core[0].reshape(ncore, RANK, D3).transpose(0, 2, 1)
    blank = jnp.zeros_like(tail)
    tail = jnp.concatenate(
        [jnp.concatenate([tail, blank], axis=2), jnp.concatenate([blank, tail], axis=2)], axis=1
    )
    rows = table_rows(got, head, middle_core[0], tail)

    returned = lax.all_to_all(rows, "table", split_axis=0, concat_axis=0, tiled=True)

    place = lax.axis_index("dp").astype(jnp.int32).reshape(1)
    weight_grad, *others = partial_product(rows.reshape(tables * own, WIDTH), gathered, place, n_data)
    for k, other in enumerate(others, 1):
        came = lax.ppermute(other, "dp", [(i, (i + k) % n_data) for i in range(n_data)])
        weight_grad = weight_grad + came.astype(jnp.float32)

    returned, weight_grad = lax.optimization_barrier((returned, weight_grad))
    pooled = side_by_side(returned)
    return (pooled, weight_grad)


def solution(mesh):
    placed = (
        P(("dp", "table"), None, None, None),
        P(("dp", "table"), None),
        P("table", None, None),
        P("table", None, None, None),
        P("table", None, None),
        P(("dp", "table"), None),
    )
    return jax.shard_map(
        body,
        mesh=mesh,
        in_specs=placed,
        out_specs=(P(("dp", "table"), None), P("table", "dp")),
        check_vma=False,
    )
```

```python
import functools

import jax
import jax.numpy as jnp
from jax import lax
from jax.experimental import pallas as pl
from jax.experimental.pallas import tpu as pltpu
from jax.sharding import PartitionSpec as P

D1 = 8
D2 = 2
D3 = 8
RANK = 64
BAG = 2
WIDTH = D1 * D2 * D3
BLOCK = 128
FETCHES = 5


def rows_kernel(
    got_ref, first_ref, core_ref, last_ref, rows_ref,
    prefix_ref, mixed_ref, middle_ref, ids_ref, out_ref, sems, out_sems,
):
    f32 = jnp.float32
    bf16 = jnp.bfloat16
    senders, part, _ = out_ref.shape
    per_block = BLOCK // part
    blocks = senders // per_block
    groups = BLOCK // 8
    row16 = lax.broadcasted_iota(jnp.int32, (16, 128), 0)
    lane16 = lax.broadcasted_iota(jnp.int32, (16, 128), 1)
    keep = ((row16 < 8) == (lane16 < 64)).astype(bf16)
    lane = lax.broadcasted_iota(jnp.int32, (8, 128), 1) // 16

    size = core_ref.shape[0] // FETCHES
    copies = [pltpu.make_async_copy(got_ref, ids_ref, sems.at[FETCHES])]
    for f in range(FETCHES):
        part_of = pl.ds(f * size, size)
        copies.append(
            pltpu.make_async_copy(core_ref.at[part_of], middle_ref.at[part_of], sems.at[f])
        )
    for copy in copies:
        copy.start()
    for copy in copies:
        copy.wait()

    def index(i, word, sample):
        return ids_ref[i * per_block + sample // part, word // BAG, word % BAG, sample % part]

    def prefixes(i, g):
        for n in range(0, 8, 4):
            at = g * 64 + n * 8
            for j in range(BAG):
                left, right = [], []
                for m in (n, n + 2):
                    pair = (m * groups + g, (m + 1) * groups + g)
                    two = [first_ref[index(i, j, a)] for a in pair]
                    left.append(jnp.concatenate(two, axis=0).astype(bf16) * keep)
                    two = [middle_ref[index(i, 2 + j, a)] for a in pair]
                    right.append(jnp.concatenate(two, axis=0))
                product = jnp.dot(
                    jnp.concatenate(left, axis=0),
                    jnp.concatenate(right, axis=1),
                    preferred_element_type=f32,
                ).astype(bf16)
                prefix_ref[at : at + 16, j * 128 : j * 128 + 128] = product[:16, :128]
                prefix_ref[at + 16 : at + 32, j * 128 : j * 128 + 128] = product[16:, 128:]

    def contract(i, g):
        tails = [
            jnp.concatenate(
                [last_ref[index(i, 4 + j, n * groups + e)] for e in (g, g + 1) for n in range(8)],
                axis=0,
            )
            for j in range(BAG)
        ]
        product = lax.dot_general(
            prefix_ref[g * 64 : g * 64 + 128, :],
            jnp.concatenate(tails, axis=1),
            (((1,), (1,)), ((), ())),
            preferred_element_type=f32,
        )
        for e in range(2):
            own = product[e * 64 : e * 64 + 64, e * 128 : e * 128 + 128]
            mixed = own[:8]
            for n in range(1, 8):
                mixed = jnp.where(lane == n, own[n * 8 : n * 8 + 8], mixed)
            mixed_ref[(g + e) * 8 : (g + e) * 8 + 8, :] = mixed

    def arrange(i, h):
        parts = [mixed_ref[pl.ds(h * 8 + a, 8, stride=8), :] for a in range(8)]
        for k in (1, 2, 4):
            low = (lane & k) == 0
            moved = list(parts)
            for a in range(8):
                if a & k == 0:
                    p, q = parts[a], parts[a + k]
                    moved[a] = jnp.where(low, p, pltpu.roll(q, 16 * k, 1))
                    moved[a + k] = jnp.where(low, pltpu.roll(p, 128 - 16 * k, 1), q)
            parts = moved
        for n in range(8):
            at = n * groups + h
            out_ref[i * per_block + at // part, at % part : at % part + 8, :] = parts[n].astype(bf16)

    def step(now, before, earlier):
        if earlier is not None:
            for h in range(0, groups, 8):
                arrange(earlier, h)
        for g in range(0, groups, 2):
            if before is not None:
                contract(before, g)
            if now is not None:
                prefixes(now, g)
                prefixes(now, g + 1)

    def turn(i, carry):
        step(i, i - 1, i - 2)
        return carry

    def leave(number, first, count):
        blocks_of = pl.ds(first, count)
        return pltpu.make_async_copy(out_ref.at[blocks_of], rows_ref.at[blocks_of], out_sems.at[number])

    step(0, None, None)
    step(1, 0, None)
    lax.fori_loop(2, blocks, turn, 0, unroll=5)
    leave(0, 0, blocks - 2).start()
    step(None, blocks - 1, blocks - 2)
    step(None, None, blocks - 1)
    leave(1, blocks - 2, 2).start()
    leave(0, 0, blocks - 2).wait()
    leave(1, blocks - 2, 2).wait()


def table_rows(got, head, middle, tail):
    senders, own = got.shape[0], got.shape[-1]
    lookups = senders * own * BAG
    vmem = pl.BlockSpec(memory_space=pltpu.VMEM)
    return pl.pallas_call(
        rows_kernel,
        out_shape=jax.ShapeDtypeStruct((senders, own, WIDTH), jnp.bfloat16),
        in_specs=[pl.BlockSpec(memory_space=pl.ANY), vmem, pl.BlockSpec(memory_space=pl.ANY), vmem],
        out_specs=pl.BlockSpec(memory_space=pl.ANY),
        scratch_shapes=[
            pltpu.VMEM((BLOCK * 8, 256), jnp.bfloat16),
            pltpu.VMEM((BLOCK, 128), jnp.float32),
            pltpu.VMEM(middle.shape, middle.dtype),
            pltpu.SMEM(got.shape, got.dtype),
            pltpu.VMEM((senders, own, WIDTH), jnp.bfloat16),
            pltpu.SemaphoreType.DMA((FETCHES + 1,)),
            pltpu.SemaphoreType.DMA((2,)),
        ],
        compiler_params=pltpu.CompilerParams(vmem_limit_bytes=50 << 20),
        cost_estimate=pl.CostEstimate(
            flops=lookups * 2000000, bytes_accessed=6 << 20, transcendentals=0
        ),
    )(got, head, middle, tail)


def product_kernel(place_ref, rows_ref, grad_ref, own_ref, *refs):
    others, (held_ref, total_ref, sems) = refs[:-3], refs[-3:]
    chunks, size, _ = held_ref.shape
    copies = []
    for i in range(chunks):
        source = grad_ref.at[pl.ds(i * size, size)]
        copies.append(pltpu.make_async_copy(source, held_ref.at[i], sems.at[i]))
        copies[-1].start()
    for i in range(chunks):
        copies[i].wait()
        value = lax.dot_general(
            rows_ref[i * size : (i + 1) * size, :],
            held_ref[i],
            (((0,), (0,)), ((), ())),
            preferred_element_type=jnp.float32,
        )
        if i == 0:
            total_ref[...] = value
        else:
            total_ref[...] += value
    columns = own_ref.shape[1]
    parts = len(others) + 1
    for k in range(parts):
        at = pl.multiple_of(lax.rem(place_ref[0] + k, parts) * columns, columns)
        block = total_ref[:, pl.ds(at, columns)]
        if k == 0:
            own_ref[...] = block
        else:
            others[k - 1][...] = block.astype(jnp.bfloat16)


def partial_product(rows, grad, place, parts):
    samples, width = rows.shape
    hidden_units = grad.shape[1]
    size = min(samples, 512)
    vmem = pl.BlockSpec(memory_space=pltpu.VMEM)
    return pl.pallas_call(
        product_kernel,
        out_shape=[jax.ShapeDtypeStruct((width, hidden_units // parts), jnp.float32)]
        + [jax.ShapeDtypeStruct((width, hidden_units // parts), jnp.bfloat16)] * (parts - 1),
        in_specs=[
            pl.BlockSpec(memory_space=pltpu.SMEM),
            vmem,
            pl.BlockSpec(memory_space=pltpu.HBM),
        ],
        out_specs=[vmem] * parts,
        scratch_shapes=[
            pltpu.VMEM((samples // size, size, hidden_units), grad.dtype),
            pltpu.VMEM((width, hidden_units), jnp.float32),
            pltpu.SemaphoreType.DMA((samples // size,)),
        ],
        compiler_params=pltpu.CompilerParams(vmem_limit_bytes=50 << 20),
        cost_estimate=pl.CostEstimate(
            flops=2 * samples * width * hidden_units,
            bytes_accessed=2 * samples * (width + hidden_units),
            transcendentals=0,
        ),
    )(place, rows, grad)


def mask_kernel(ids_ref, lengths_ref, out_ref, *, unused):
    slot = lax.broadcasted_iota(jnp.int32, ids_ref.shape[:1] + ids_ref.shape[2:], 1)
    out_ref[:, 1:] = ids_ref[:, 1:]
    out_ref[:, 0] = jnp.where(slot < lengths_ref[...][:, None, :], ids_ref[:, 0], unused)


def masked(ids, lengths, unused):
    vmem = pl.BlockSpec(memory_space=pltpu.VMEM)
    return pl.pallas_call(
        functools.partial(mask_kernel, unused=unused),
        out_shape=jax.ShapeDtypeStruct(ids.shape, ids.dtype),
        in_specs=[vmem, vmem],
        out_specs=vmem,
    )(ids, lengths)


def beside_kernel(blocks_ref, out_ref, rows_ref, sems):
    tables, _, width = blocks_ref.shape
    pieces, size, _ = rows_ref.shape
    copies = []
    for p in range(pieces):
        for t in range(tables):
            rows_ref[p, :, t * width : (t + 1) * width] = blocks_ref[t, p * size : (p + 1) * size]
        target = out_ref.at[pl.ds(p * size, size)]
        copies.append(pltpu.make_async_copy(rows_ref.at[p], target, sems.at[p]))
        copies[-1].start()
    for copy in copies:
        copy.wait()


def side_by_side(blocks):
    tables, own, width = blocks.shape
    pieces = own // 16
    return pl.pallas_call(
        beside_kernel,
        out_shape=jax.ShapeDtypeStruct((own, tables * width), blocks.dtype),
        in_specs=[pl.BlockSpec(memory_space=pltpu.VMEM)],
        out_specs=pl.BlockSpec(memory_space=pl.ANY),
        scratch_shapes=[
            pltpu.VMEM((pieces, own // pieces, tables * width), blocks.dtype),
            pltpu.SemaphoreType.DMA((pieces,)),
        ],
        compiler_params=pltpu.CompilerParams(vmem_limit_bytes=4 << 20),
    )(blocks)


def body(core_ids, bag_lengths, first_core, middle_core, last_core, grad_hidden):
    own, tables = bag_lengths.shape
    ncore = first_core.shape[1]
    n_data = lax.axis_size("dp")

    gathered = lax.all_gather(grad_hidden, "table", axis=0, tiled=True)

    sent = masked(jnp.transpose(core_ids, (1, 2, 3, 0)), jnp.transpose(bag_lengths), ncore)
    got = lax.all_to_all(sent, "table", split_axis=0, concat_axis=0, tiled=True)

    head = first_core[0].reshape(ncore, D1, RANK).astype(jnp.float32)
    head = jnp.pad(jnp.concatenate([head, head], axis=2), ((0, 8), (0, 0), (0, 0)))
    tail = last_core[0].reshape(ncore, RANK, D3).transpose(0, 2, 1)
    blank = jnp.zeros_like(tail)
    tail = jnp.concatenate(
        [jnp.concatenate([tail, blank], axis=2), jnp.concatenate([blank, tail], axis=2)], axis=1
    )
    rows = table_rows(got, head, middle_core[0], tail)

    returned = lax.all_to_all(rows, "table", split_axis=0, concat_axis=0, tiled=True)

    place = lax.axis_index("dp").astype(jnp.int32).reshape(1)
    weight_grad, *others = partial_product(rows.reshape(tables * own, WIDTH), gathered, place, n_data)
    for k, other in enumerate(others, 1):
        came = lax.ppermute(other, "dp", [(i, (i + k) % n_data) for i in range(n_data)])
        weight_grad = weight_grad + came.astype(jnp.float32)

    returned, weight_grad = lax.optimization_barrier((returned, weight_grad))
    pooled = side_by_side(returned)
    return (pooled, weight_grad)


def solution(mesh):
    placed = (
        P(("dp", "table"), None, None, None),
        P(("dp", "table"), None),
        P("table", None, None),
        P("table", None, None, None),
        P("table", None, None),
        P(("dp", "table"), None),
    )
    return jax.shard_map(
        body,
        mesh=mesh,
        in_specs=placed,
        out_specs=(P(("dp", "table"), None), P("table", "dp")),
        check_vma=False,
    )
```

```python
import functools

import jax
import jax.numpy as jnp
from jax import lax
from jax.experimental import pallas as pl
from jax.experimental.pallas import tpu as pltpu
from jax.sharding import PartitionSpec as P

D1 = 8
D2 = 2
D3 = 8
RANK = 64
BAG = 2
WIDTH = D1 * D2 * D3
BLOCK = 128
FETCHES = 5


def rows_kernel(
    got_ref, first_ref, core_ref, last_ref, rows_ref,
    prefix_ref, mixed_ref, middle_ref, ids_ref, out_ref, sems, out_sems,
):
    f32 = jnp.float32
    bf16 = jnp.bfloat16
    senders, part, _ = out_ref.shape
    per_block = BLOCK // part
    blocks = senders // per_block
    groups = BLOCK // 8
    row16 = lax.broadcasted_iota(jnp.int32, (16, 128), 0)
    lane16 = lax.broadcasted_iota(jnp.int32, (16, 128), 1)
    keep = ((row16 < 8) == (lane16 < 64)).astype(bf16)
    lane = lax.broadcasted_iota(jnp.int32, (8, 128), 1) // 16

    size = core_ref.shape[0] // FETCHES
    copies = [pltpu.make_async_copy(got_ref, ids_ref, sems.at[FETCHES])]
    for f in range(FETCHES):
        part_of = pl.ds(f * size, size)
        copies.append(
            pltpu.make_async_copy(core_ref.at[part_of], middle_ref.at[part_of], sems.at[f])
        )
    for copy in copies:
        copy.start()
    for copy in copies:
        copy.wait()

    def index(i, word, sample):
        return ids_ref[i * per_block + sample // part, word // BAG, word % BAG, sample % part]

    def prefixes(i, g):
        for n in range(0, 8, 4):
            at = g * 64 + n * 8
            for j in range(BAG):
                left, right = [], []
                for m in (n, n + 2):
                    pair = (m * groups + g, (m + 1) * groups + g)
                    two = [first_ref[index(i, j, a)] for a in pair]
                    left.append(jnp.concatenate(two, axis=0).astype(bf16) * keep)
                    two = [middle_ref[index(i, 2 + j, a)] for a in pair]
                    right.append(jnp.concatenate(two, axis=0))
                product = jnp.dot(
                    jnp.concatenate(left, axis=0),
                    jnp.concatenate(right, axis=1),
                    preferred_element_type=f32,
                ).astype(bf16)
                prefix_ref[at : at + 16, j * 128 : j * 128 + 128] = product[:16, :128]
                prefix_ref[at + 16 : at + 32, j * 128 : j * 128 + 128] = product[16:, 128:]

    def contract(i, g):
        tails = [
            jnp.concatenate(
                [last_ref[index(i, 4 + j, n * groups + e)] for e in (g, g + 1) for n in range(8)],
                axis=0,
            )
            for j in range(BAG)
        ]
        product = lax.dot_general(
            prefix_ref[g * 64 : g * 64 + 128, :],
            jnp.concatenate(tails, axis=1),
            (((1,), (1,)), ((), ())),
            preferred_element_type=f32,
        )
        for e in range(2):
            own = product[e * 64 : e * 64 + 64, e * 128 : e * 128 + 128]
            mixed = own[:8]
            for n in range(1, 8):
                mixed = jnp.where(lane == n, own[n * 8 : n * 8 + 8], mixed)
            mixed_ref[(g + e) * 8 : (g + e) * 8 + 8, :] = mixed

    def arrange(i, h):
        parts = [mixed_ref[pl.ds(h * 8 + a, 8, stride=8), :] for a in range(8)]
        for k in (1, 2, 4):
            low = (lane & k) == 0
            moved = list(parts)
            for a in range(8):
                if a & k == 0:
                    p, q = parts[a], parts[a + k]
                    moved[a] = jnp.where(low, p, pltpu.roll(q, 16 * k, 1))
                    moved[a + k] = jnp.where(low, pltpu.roll(p, 128 - 16 * k, 1), q)
            parts = moved
        for n in range(8):
            at = n * groups + h
            out_ref[i * per_block + at // part, at % part : at % part + 8, :] = parts[n].astype(bf16)

    def step(now, before, earlier):
        if earlier is not None:
            for h in range(0, groups, 8):
                arrange(earlier, h)
        for g in range(0, groups, 2):
            if before is not None:
                contract(before, g)
            if now is not None:
                prefixes(now, g)
                prefixes(now, g + 1)

    def turn(i, carry):
        step(i, i - 1, i - 2)
        return carry

    def leave(number, first, count):
        blocks_of = pl.ds(first, count)
        return pltpu.make_async_copy(out_ref.at[blocks_of], rows_ref.at[blocks_of], out_sems.at[number])

    step(0, None, None)
    step(1, 0, None)
    lax.fori_loop(2, blocks, turn, 0, unroll=5)
    leave(0, 0, blocks - 2).start()
    step(None, blocks - 1, blocks - 2)
    step(None, None, blocks - 1)
    leave(1, blocks - 2, 2).start()
    leave(0, 0, blocks - 2).wait()
    leave(1, blocks - 2, 2).wait()


def table_rows(got, head, middle, tail):
    senders, own = got.shape[0], got.shape[-1]
    lookups = senders * own * BAG
    vmem = pl.BlockSpec(memory_space=pltpu.VMEM)
    return pl.pallas_call(
        rows_kernel,
        out_shape=jax.ShapeDtypeStruct((senders, own, WIDTH), jnp.bfloat16),
        in_specs=[pl.BlockSpec(memory_space=pl.ANY), vmem, pl.BlockSpec(memory_space=pl.ANY), vmem],
        out_specs=pl.BlockSpec(memory_space=pl.ANY),
        scratch_shapes=[
            pltpu.VMEM((BLOCK * 8, 256), jnp.bfloat16),
            pltpu.VMEM((BLOCK, 128), jnp.float32),
            pltpu.VMEM(middle.shape, middle.dtype),
            pltpu.SMEM(got.shape, got.dtype),
            pltpu.VMEM((senders, own, WIDTH), jnp.bfloat16),
            pltpu.SemaphoreType.DMA((FETCHES + 1,)),
            pltpu.SemaphoreType.DMA((2,)),
        ],
        compiler_params=pltpu.CompilerParams(vmem_limit_bytes=50 << 20),
        cost_estimate=pl.CostEstimate(
            flops=lookups * 2000000, bytes_accessed=6 << 20, transcendentals=0
        ),
    )(got, head, middle, tail)


def product_kernel(place_ref, rows_ref, grad_ref, own_ref, *refs):
    others, (held_ref, total_ref, sems) = refs[:-3], refs[-3:]
    chunks, size, _ = held_ref.shape
    copies = []
    for i in range(chunks):
        source = grad_ref.at[pl.ds(i * size, size)]
        copies.append(pltpu.make_async_copy(source, held_ref.at[i], sems.at[i]))
        copies[-1].start()
    for i in range(chunks):
        copies[i].wait()
        value = lax.dot_general(
            rows_ref[i * size : (i + 1) * size, :],
            held_ref[i],
            (((0,), (0,)), ((), ())),
            preferred_element_type=jnp.float32,
        )
        if i == 0:
            total_ref[...] = value
        else:
            total_ref[...] += value
    columns = own_ref.shape[1]
    parts = len(others) + 1
    for k in range(parts):
        at = pl.multiple_of(lax.rem(place_ref[0] + k, parts) * columns, columns)
        block = total_ref[:, pl.ds(at, columns)]
        if k == 0:
            own_ref[...] = block
        else:
            others[k - 1][...] = block.astype(jnp.bfloat16)


def partial_product(rows, grad, place, parts):
    samples, width = rows.shape
    hidden_units = grad.shape[1]
    size = min(samples, 256)
    vmem = pl.BlockSpec(memory_space=pltpu.VMEM)
    return pl.pallas_call(
        product_kernel,
        out_shape=[jax.ShapeDtypeStruct((width, hidden_units // parts), jnp.float32)]
        + [jax.ShapeDtypeStruct((width, hidden_units // parts), jnp.bfloat16)] * (parts - 1),
        in_specs=[
            pl.BlockSpec(memory_space=pltpu.SMEM),
            vmem,
            pl.BlockSpec(memory_space=pltpu.HBM),
        ],
        out_specs=[vmem] * parts,
        scratch_shapes=[
            pltpu.VMEM((samples // size, size, hidden_units), grad.dtype),
            pltpu.VMEM((width, hidden_units), jnp.float32),
            pltpu.SemaphoreType.DMA((samples // size,)),
        ],
        compiler_params=pltpu.CompilerParams(vmem_limit_bytes=50 << 20),
        cost_estimate=pl.CostEstimate(
            flops=2 * samples * width * hidden_units,
            bytes_accessed=2 * samples * (width + hidden_units),
            transcendentals=0,
        ),
    )(place, rows, grad)


def mask_kernel(ids_ref, lengths_ref, out_ref, *, unused):
    slot = lax.broadcasted_iota(jnp.int32, ids_ref.shape[:1] + ids_ref.shape[2:], 1)
    out_ref[:, 1:] = ids_ref[:, 1:]
    out_ref[:, 0] = jnp.where(slot < lengths_ref[...][:, None, :], ids_ref[:, 0], unused)


def masked(ids, lengths, unused):
    vmem = pl.BlockSpec(memory_space=pltpu.VMEM)
    return pl.pallas_call(
        functools.partial(mask_kernel, unused=unused),
        out_shape=jax.ShapeDtypeStruct(ids.shape, ids.dtype),
        in_specs=[vmem, vmem],
        out_specs=vmem,
    )(ids, lengths)


def beside_kernel(blocks_ref, out_ref, rows_ref, sems):
    tables, _, width = blocks_ref.shape
    pieces, size, _ = rows_ref.shape
    copies = []
    for p in range(pieces):
        for t in range(tables):
            rows_ref[p, :, t * width : (t + 1) * width] = blocks_ref[t, p * size : (p + 1) * size]
        target = out_ref.at[pl.ds(p * size, size)]
        copies.append(pltpu.make_async_copy(rows_ref.at[p], target, sems.at[p]))
        copies[-1].start()
    for copy in copies:
        copy.wait()


def side_by_side(blocks):
    tables, own, width = blocks.shape
    pieces = own // 16
    return pl.pallas_call(
        beside_kernel,
        out_shape=jax.ShapeDtypeStruct((own, tables * width), blocks.dtype),
        in_specs=[pl.BlockSpec(memory_space=pltpu.VMEM)],
        out_specs=pl.BlockSpec(memory_space=pl.ANY),
        scratch_shapes=[
            pltpu.VMEM((pieces, own // pieces, tables * width), blocks.dtype),
            pltpu.SemaphoreType.DMA((pieces,)),
        ],
        compiler_params=pltpu.CompilerParams(vmem_limit_bytes=4 << 20),
    )(blocks)


def body(core_ids, bag_lengths, first_core, middle_core, last_core, grad_hidden):
    own, tables = bag_lengths.shape
    ncore = first_core.shape[1]
    n_data = lax.axis_size("dp")

    gathered = lax.all_gather(grad_hidden, "table", axis=0, tiled=True)

    sent = masked(jnp.transpose(core_ids, (1, 2, 3, 0)), jnp.transpose(bag_lengths), ncore)
    got = lax.all_to_all(sent, "table", split_axis=0, concat_axis=0, tiled=True)

    head = first_core[0].reshape(ncore, D1, RANK).astype(jnp.float32)
    head = jnp.pad(jnp.concatenate([head, head], axis=2), ((0, 8), (0, 0), (0, 0)))
    tail = last_core[0].reshape(ncore, RANK, D3).transpose(0, 2, 1)
    blank = jnp.zeros_like(tail)
    tail = jnp.concatenate(
        [jnp.concatenate([tail, blank], axis=2), jnp.concatenate([blank, tail], axis=2)], axis=1
    )
    rows = table_rows(got, head, middle_core[0], tail)

    returned = lax.all_to_all(rows, "table", split_axis=0, concat_axis=0, tiled=True)

    place = lax.axis_index("dp").astype(jnp.int32).reshape(1)
    weight_grad, *others = partial_product(rows.reshape(tables * own, WIDTH), gathered, place, n_data)
    for k, other in enumerate(others, 1):
        came = lax.ppermute(other, "dp", [(i, (i + k) % n_data) for i in range(n_data)])
        weight_grad = weight_grad + came.astype(jnp.float32)

    returned, weight_grad = lax.optimization_barrier((returned, weight_grad))
    pooled = side_by_side(returned)
    return (pooled, weight_grad)


def solution(mesh):
    placed = (
        P(("dp", "table"), None, None, None),
        P(("dp", "table"), None),
        P("table", None, None),
        P("table", None, None, None),
        P("table", None, None),
        P(("dp", "table"), None),
    )
    return jax.shard_map(
        body,
        mesh=mesh,
        in_specs=placed,
        out_specs=(P(("dp", "table"), None), P("table", "dp")),
        check_vma=False,
    )
```
